512 devices in a mesh: seq: 64 (over x, z), head: 8 (over y, core).
Axes of the slice: x: 4, y: 4, z: 16, core: 2. Of those that a mesh axis runs over, the one named last changes fastest.
Arguments:
- lin_query: bfloat16 [32768, 4096], P('seq', 'head'), may hold values from -6 to 6
- lin_key: bfloat16 [32768, 4096], P('seq', 'head'), may hold values from -6 to 6
- lin_value: bfloat16 [32768, 4096], P('seq', 'head'), may hold values from -54 to 54
- lin_gate: bfloat16 [32768, 4096], P('seq', 'head'), may hold values from -6 to 6
- log_decay: float32 [32768, 32], P('seq', 'head'), as said below
- norm_gain: float32 [4096], P('head'), may hold values from 0.1 to 1.9
- soft_query: bfloat16 [32768, 4096], P('seq', 'head'), may hold values from -4.5 to 4.5
- soft_key: bfloat16 [32768, 1024], P('seq', 'head'), may hold values from -4.5 to 4.5
- soft_value: bfloat16 [32768, 1024], P('seq', 'head'), may hold values from -6 to 6
- doc_ids: int32 [256], replicated, may hold values from 0 to 31, never falling along the last dimension, each value on 1 to 29 neighbouring positions
Outputs:
- lin_out: bfloat16 [32768, 4096], P('seq', 'head')
- soft_out: bfloat16 [32768, 4096], P('seq', 'head')
The draws below stay inside these ranges and needn't reach their ends.
Inputs may be any that keep to these rules, and one draw needn't show every extreme that they name: `log_decay`: every entry is below zero. `doc_ids`: never falling along the window; every document covers 1 to 29 mask blocks, one exactly 29.
All inputs are finite; a program needn't handle non-finite values.
Results may differ from the reference program's by a relative error of at most 0.004.
Values may be sent and summed in bfloat16 or wider, within the bound.
No kernel may reach another device: no remote copies, remote signals or barrier semaphores. Data moves between devices by JAX's collectives and lax.ppermute only.
A program may use at most 128 MiB of HBM per device.

```python
import math
import jax
import jax.numpy as jnp
import numpy as np
from jax import lax

HD = 128
TOK_DEV = 512
BLK = 256
MBLK = 128
DOC_MOST = 29
HEAD_TOTAL = 32
KV_HEADS = 8
WINDOW_TOKENS = 32768
NBLK = 256
DOCS = 32


def draw_log_decay(key, part):
    key_collection = jax.random.split(key, 7)
    fast_share = 0.5
    is_fast = jax.random.uniform(key_collection[0], (HEAD_TOTAL,)) < fast_share
    fast_rate = jnp.exp(jax.random.uniform(key_collection[1], (HEAD_TOTAL,), minval=math.log(5.0 / BLK), maxval=math.log(8.0 / BLK)))
    slow_rate = jnp.exp(jax.random.uniform(key_collection[2], (HEAD_TOTAL,), minval=math.log(0.1), maxval=math.log(0.4))) * (math.log(10.0) / WINDOW_TOKENS)
    head_rate = jnp.where(is_fast, fast_rate, slow_rate)
    dev_factor = jax.random.uniform(key_collection[3], (WINDOW_TOKENS // TOK_DEV, 1), minval=0.6, maxval=1.4)
    dev_factor = jnp.repeat(dev_factor, TOK_DEV, axis=0)
    jitter = jax.random.uniform(key_collection[4], (WINDOW_TOKENS, HEAD_TOTAL), minval=0.5, maxval=1.5)
    final_output = -head_rate[None, :] * dev_factor * jitter
    token_positions = jnp.arange(WINDOW_TOKENS)
    packet_position = jax.random.randint(key_collection[5], (2,), 0, WINDOW_TOKENS)
    packet_weight_loss = jax.random.uniform(key_collection[6], (2, HEAD_TOTAL), minval=0.2, maxval=0.35)
    for packet_index in range(2):
        at_packet = (token_positions == packet_position[packet_index])[:, None]
        final_output = final_output + jnp.where(at_packet, jnp.log(1.0 - packet_weight_loss[packet_index])[None, :], 0.0)
    return final_output.astype(jnp.float32)


def draw_lin_value(key, part):
    first_key, second_key = jax.random.split(key, 2)
    base = jnp.clip(jax.random.normal(first_key, (WINDOW_TOKENS, HEAD_TOTAL * HD)), -6.0, 6.0)
    head_place = jnp.arange(HEAD_TOTAL, dtype=jnp.float32) / max(HEAD_TOTAL - 1, 1)
    head_scale = jnp.exp(math.log(3.0) * head_place) * jnp.exp(jax.random.uniform(second_key, (HEAD_TOTAL,), minval=0.0, maxval=math.log(3.0)))
    column_scale = jnp.repeat(head_scale, HD)
    return (base * column_scale[None, :]).astype(jnp.bfloat16)


def soft_pair(key):
    base_key = jax.random.fold_in(key, 7)
    key_collection = jax.random.split(base_key, 2)
    query_matrix = jnp.clip(jax.random.normal(key_collection[0], (WINDOW_TOKENS, HEAD_TOTAL * HD)), -4.5, 4.5)
    key_rows = jnp.clip(jax.random.normal(key_collection[1], (WINDOW_TOKENS, KV_HEADS * HD)), -4.5, 4.5)
    return (query_matrix, key_rows)


def draw_soft_query(key, part):
    return soft_pair(key)[0].astype(jnp.bfloat16)


def draw_soft_key(key, part):
    return soft_pair(key)[1].astype(jnp.bfloat16)


def levels(rng, shape, cuts, least, top_value):
    def one(axis_at, blocks):
        heights = jax.random.uniform(jax.random.fold_in(jax.random.fold_in(rng, 6), axis_at), (blocks,), jnp.float32, least / len(cuts), top_value / len(cuts))
        return jnp.repeat(jnp.exp(heights), shape[axis_at] // blocks).reshape((-1,) + (1,) * (len(shape) - axis_at - 1))

    loudness = one(*cuts[0])
    for cut in cuts[1:]:
        loudness = loudness * one(*cut)
    return loudness


def profile(count, total, reach, skew):
    loads = [(1 << 20) // math.isqrt(rank ** skew) + 1 for rank in range(2, count + 1)]
    spare, counts = total - reach - (count - 1), [1] * (count - 1)
    while spare > 0:
        free = [i for i in range(count - 1) if counts[i] < reach]
        pool, budget = sum([loads[i] for i in free]), spare
        for i in free:
            extra = min(reach - counts[i], max(1, budget * loads[i] // pool), spare)
            counts[i] = counts[i] + extra
            spare = spare - extra
    return np.array([reach] + counts)


def ragged_sizes(rng, count, total, most, skew):
    if count == 2:
        one = jax.random.randint(rng, (), max(1, total - most), min(most, total - 1) + 1)
        return jnp.stack([one, total - one])
    tallies = jnp.asarray(profile(count, total, most, skew), jnp.int32)
    pairs = (count - 1) // 2
    donor, sink = tallies[1:1 + 2 * pairs:2], tallies[2:2 + 2 * pairs:2]
    slack = jnp.minimum(donor - 1, most - sink)
    moved = jax.random.randint(jax.random.fold_in(rng, 1), (pairs,), 0, 1 << 20) % (slack + 1)
    tallies = tallies.at[1:1 + 2 * pairs:2].set(donor - moved).at[2:2 + 2 * pairs:2].set(sink + moved)
    return tallies[jax.random.permutation(jax.random.fold_in(rng, 2), count)]


def normal_values(key, dims, spread, limit, cuts=(), kind=jnp.bfloat16):
    array = spread * jax.random.normal(key, dims, jnp.float32)
    if cuts:
        array = array * levels(key, dims, cuts, -0.22, 0.18)
    return jnp.clip(array, -limit, limit).astype(kind)


def setup_inputs(seed: int = 0) -> dict:
    seeds = jax.random.split(jax.random.key(seed), 11)
    return {
        "lin_query": normal_values(seeds[0], (WINDOW_TOKENS, HEAD_TOTAL * HD), 1.0, 6.0, ((0, 64), (1, 8))),
        "lin_key": normal_values(seeds[1], (WINDOW_TOKENS, HEAD_TOTAL * HD), 1.0, 6.0, ((0, 64), (1, 8))),
        "lin_value": draw_lin_value(jax.random.fold_in(seeds[10], 71), 0),
        "lin_gate": normal_values(seeds[3], (WINDOW_TOKENS, HEAD_TOTAL * HD), 1.5, 6.0, ((0, 64), (1, 8))),
        "log_decay": draw_log_decay(jax.random.fold_in(seeds[10], 71), 0),
        "norm_gain": jnp.clip(1.0 + 0.18 * jax.random.normal(seeds[5], (HEAD_TOTAL * HD,), jnp.float32), 0.1, 1.9),
        "soft_query": draw_soft_query(jax.random.fold_in(seeds[10], 71), 0),
        "soft_key": draw_soft_key(jax.random.fold_in(seeds[10], 71), 0),
        "soft_value": normal_values(seeds[8], (WINDOW_TOKENS, KV_HEADS * HD), 1.0, 6.0, ((0, 64), (1, 8))),
        "doc_ids": jnp.searchsorted(jnp.cumsum(ragged_sizes(seeds[9], DOCS, NBLK, DOC_MOST, 2)), jnp.arange(NBLK), side="right").astype(jnp.int32),
    }


eps = 1e-06

def lightning_ref(lin_query, lin_key, lin_value, lin_gate, log_decay, norm_gain):
    block_count = WINDOW_TOKENS // BLK
    query_matrix = lin_query.reshape(block_count, BLK, HEAD_TOTAL, HD)
    key_rows = lin_key.reshape(block_count, BLK, HEAD_TOTAL, HD)
    values = lin_value.reshape(block_count, BLK, HEAD_TOTAL, HD)
    cumulative = jnp.cumsum(log_decay.reshape(block_count, BLK, HEAD_TOTAL), axis=1)
    causal = lax.broadcasted_iota(jnp.int32, (BLK, BLK), 0) >= lax.broadcasted_iota(jnp.int32, (BLK, BLK), 1)
    high = lax.Precision.HIGHEST

    def one_block(carried, block_item):
        block_q, block_k, block_v, block_cum = block_item
        query_f = block_q.astype(jnp.float32)
        value_f = block_v.astype(jnp.float32)
        scores = jnp.einsum('tha,sha->hts', query_f, block_k.astype(jnp.float32), precision=high)
        cum_heads = block_cum.T
        gap_sums = cum_heads[:, :, None] - cum_heads[:, None, :]
        weight = jnp.exp(jnp.where(causal[None], gap_sums, -1e+30))
        mixed_scores = (scores * weight).astype(jnp.bfloat16)
        mixed_scores = lax.optimization_barrier(mixed_scores).astype(jnp.float32)
        intra_term = jnp.einsum('hts,sha->tha', mixed_scores, value_f, precision=high)
        scaled_q = query_f * jnp.exp(block_cum)[:, :, None]
        inter_term = jnp.einsum('tha,hac->thc', scaled_q, carried, precision=high)
        block_total = block_cum[-1]
        weighted = block_k.astype(jnp.float32) * jnp.exp(block_total[None, :] - block_cum)[:, :, None]
        local_state = jnp.einsum('sha,shc->hac', weighted, value_f, precision=high)
        carried = jnp.exp(block_total)[:, None, None] * carried + local_state
        return (carried, intra_term + inter_term)
    start_state = jnp.zeros((HEAD_TOTAL, HD, HD), jnp.float32)
    _, raw_out = lax.scan(one_block, start_state, (query_matrix, key_rows, values, cumulative))
    raw_out = raw_out.reshape(WINDOW_TOKENS, HEAD_TOTAL * HD)
    mean_sq = lax.optimization_barrier(jnp.mean(raw_out * raw_out, axis=1))
    norm_scale = lax.rsqrt(mean_sq + eps)
    gated = raw_out * norm_scale[:, None] * norm_gain[None, :] * jax.nn.sigmoid(lin_gate.astype(jnp.float32))
    return gated.astype(jnp.bfloat16)

def softmax_ref(soft_query, soft_key, soft_value, doc_ids):
    query_block = min(512, WINDOW_TOKENS)
    key_span = min(DOC_MOST * MBLK + query_block, WINDOW_TOKENS)
    token_docs = jnp.repeat(doc_ids, MBLK)
    group_size = HEAD_TOTAL // KV_HEADS
    high = lax.Precision.HIGHEST

    def one_range(start):
        key_start = jnp.maximum(start + query_block - key_span, 0)
        query_matrix = lax.dynamic_slice_in_dim(soft_query, start, query_block, 0).reshape(query_block, HEAD_TOTAL, HD).astype(jnp.float32)
        key_rows = lax.dynamic_slice_in_dim(soft_key, key_start, key_span, 0).reshape(key_span, KV_HEADS, HD).astype(jnp.float32)
        values = lax.dynamic_slice_in_dim(soft_value, key_start, key_span, 0).reshape(key_span, KV_HEADS, HD).astype(jnp.float32)
        key_rows = jnp.repeat(key_rows, group_size, axis=1)
        values = jnp.repeat(values, group_size, axis=1)
        query_pos = start + lax.iota(jnp.int32, query_block)
        key_pos = key_start + lax.iota(jnp.int32, key_span)
        query_docs = lax.dynamic_slice_in_dim(token_docs, start, query_block, 0)
        key_docs = lax.dynamic_slice_in_dim(token_docs, key_start, key_span, 0)
        allowed = (key_pos[None, :] <= query_pos[:, None]) & (key_docs[None, :] == query_docs[:, None])
        scores = jnp.einsum('tha,sha->hts', query_matrix, key_rows, precision=high) * HD ** (-0.5)
        scores = jnp.where(allowed[None], scores, -1e+30)
        row_max = lax.optimization_barrier(jnp.max(scores, axis=-1))
        probs = jnp.where(allowed[None], jnp.exp(scores - row_max[:, :, None]), 0.0)
        row_total = lax.optimization_barrier(jnp.sum(probs, axis=-1))
        probability_rows = lax.optimization_barrier(probs.astype(jnp.bfloat16)).astype(jnp.float32)
        mixed = jnp.einsum('hts,sha->tha', probability_rows, values, precision=high)
        final_output = mixed / row_total.T[:, :, None]
        return final_output.reshape(query_block, HEAD_TOTAL * HD).astype(jnp.bfloat16)
    starts = lax.iota(jnp.int32, WINDOW_TOKENS // query_block) * query_block
    pieces = lax.map(one_range, starts)
    return pieces.reshape(WINDOW_TOKENS, HEAD_TOTAL * HD)

def reference(lin_query, lin_key, lin_value, lin_gate, log_decay, norm_gain, soft_query, soft_key, soft_value, doc_ids):
    lin_out = lightning_ref(lin_query, lin_key, lin_value, lin_gate, log_decay, norm_gain)
    soft_out = softmax_ref(soft_query, soft_key, soft_value, doc_ids)
    return (lin_out, soft_out)
```

```python
import functools
import math

import jax
import jax.numpy as jnp
import numpy as np
from jax import lax
from jax.experimental import pallas as pl
from jax.experimental.pallas import tpu as pltpu
from jax.sharding import PartitionSpec as P

HD = 128
BLK = 256
MBLK = 128
DOC_MOST = 29
EPS = 1e-06
NEG = -1e30
LOG_FLOOR = -1000.0
LOG_ROWS = 16
QUAD = 4
F32 = jnp.float32
BF16 = jnp.bfloat16
VMEM_LIMIT = 48 * 1024 * 1024


def call(body, outs, operands, *, flops, moved, exps=0, scratch=(), smem=(), aliases=None):
    specs = [
        pl.BlockSpec(memory_space=pltpu.SMEM if i in smem else pltpu.VMEM)
        for i in range(len(operands))
    ]
    return pl.pallas_call(
        body,
        out_shape=outs,
        in_specs=specs,
        out_specs=jax.tree.map(lambda _: pl.BlockSpec(memory_space=pltpu.VMEM), outs),
        scratch_shapes=list(scratch),
        input_output_aliases=aliases or {},
        compiler_params=pltpu.CompilerParams(vmem_limit_bytes=VMEM_LIMIT),
        cost_estimate=pl.CostEstimate(
            flops=int(flops), bytes_accessed=int(moved), transcendentals=int(exps)
        ),
    )(*operands)


def dot(a, b, dims, precision=None):
    return lax.dot_general(
        a, b, (dims, ((), ())), preferred_element_type=F32, precision=precision
    )


def split(x):
    high = x.astype(BF16)
    return high, (x - high.astype(F32)).astype(BF16)


def block_sums(log_ref):
    rows = lax.broadcasted_iota(jnp.int32, (BLK, BLK), 0)
    cols = lax.broadcasted_iota(jnp.int32, (BLK, BLK), 1)
    tri = (rows >= cols).astype(F32)
    return [
        dot(tri, log_ref[b * BLK : (b + 1) * BLK, :], ((1,), (0,)), lax.Precision.HIGHEST)
        for b in range(log_ref.shape[0] // BLK)
    ]


def log_rows(total):
    first = total.astype(BF16).astype(F32)
    second = (total - first).astype(BF16).astype(F32)
    third = total - first - second
    row = lax.broadcasted_iota(jnp.int32, (LOG_ROWS, HD), 0)
    packed = jnp.where(row == 0, first, jnp.where(row == 1, second, jnp.where(row == 2, third, 0.0)))
    return packed.astype(BF16)


def states_body(key_ref, value_ref, log_ref, send_ref, first_ref):
    heads = key_ref.shape[1] // HD
    sums = block_sums(log_ref)
    ends = [s[BLK - 1 : BLK, :] for s in sums]
    for h in range(heads):
        lanes = slice(h * HD, (h + 1) * HD)
        state = None
        total = jnp.zeros((1, 1), F32)
        for b, cum in enumerate(sums):
            rows = slice(b * BLK, (b + 1) * BLK)
            end = ends[b][:, h : h + 1]
            weight = jnp.exp(end - cum[:, h : h + 1])
            high, low = split(key_ref[rows, lanes].astype(F32) * weight)
            value = value_ref[rows, lanes]
            local = dot(high, value, ((0,), (0,))) + dot(low, value, ((0,), (0,)))
            if b == 0:
                first_ref[h] = local
                state = local
            else:
                state = jnp.exp(end) * state + local
            total = total + end
        send_ref[h, :HD, :] = state.astype(BF16)
        total = jnp.broadcast_to(jnp.maximum(total, LOG_FLOOR), (1, HD))
        send_ref[h, HD:, :] = log_rows(total)


def local_body(query_ref, key_ref, value_ref, log_ref, first_ref, raw_ref):
    heads = key_ref.shape[1] // HD
    sums = block_sums(log_ref)
    across = [s.T for s in sums]
    rows_i = lax.broadcasted_iota(jnp.int32, (BLK, BLK), 0)
    cols_i = lax.broadcasted_iota(jnp.int32, (BLK, BLK), 1)
    causal = rows_i >= cols_i
    for b, cum in enumerate(sums):
        rows = slice(b * BLK, (b + 1) * BLK)
        for h in range(heads):
            lanes = slice(h * HD, (h + 1) * HD)
            column = cum[:, h : h + 1]
            query = query_ref[rows, lanes]
            gap = column - across[b][h : h + 1, :]
            weight = jnp.exp(jnp.where(causal, gap, NEG))
            scores = dot(query, key_ref[rows, lanes], ((1,), (1,)))
            mixed = (scores * weight).astype(BF16)
            raw = dot(mixed, value_ref[rows, lanes], ((1,), (0,)))
            if b > 0:
                high, low = split(first_ref[h])
                inter = dot(query, high, ((1,), (0,))) + dot(query, low, ((1,), (0,)))
                raw = raw + jnp.exp(column) * inter
            raw_ref[rows, lanes] = raw


def log_of(block):
    return jnp.sum(block[HD:, :].astype(F32), axis=0, keepdims=True)


def fold(parts):
    state, total = parts[0]
    for s, l in parts[1:]:
        state = jnp.exp(l) * state + s
        total = total + l
    return state, jnp.maximum(total, LOG_FLOOR)


def parts_of(got_ref):
    return [
        (got_ref[j, :HD, :].astype(F32), log_of(got_ref[j])) for j in range(got_ref.shape[0])
    ]


def group_body(got_ref, send_ref):
    state, total = fold(parts_of(got_ref))
    state = state.astype(BF16)
    rows = log_rows(total)
    for j in range(send_ref.shape[0]):
        send_ref[j, :HD, :] = state
        send_ref[j, HD:, :] = rows


def before(parts, place):
    state = jnp.zeros((HD, HD), F32)
    for j, (s, l) in enumerate(parts[:-1]):
        state = jnp.where(j < place, jnp.exp(l) * state + s, state)
    return state


def log_before(parts, place):
    total = jnp.zeros((1, HD), F32)
    for j, (_, l) in enumerate(parts[:-1]):
        total = jnp.where(j < place, total + l, total)
    return total


def enter_body(place_ref, mine_ref, line_ref, wide_ref, send_ref):
    line = parts_of(line_ref)
    wide = parts_of(wide_ref)
    state = before(wide, place_ref[1])
    entering = jnp.exp(log_before(line, place_ref[0])) * state + before(line, place_ref[0])
    for j, (s, l) in enumerate(parts_of(mine_ref)):
        send_ref[j] = entering.astype(BF16)
        entering = jnp.exp(l) * entering + s


def raw_body(query_ref, log_ref, local_ref, enter_ref, raw_ref, square_ref):
    heads = query_ref.shape[1] // HD
    sums = block_sums(log_ref)
    ahead = jnp.zeros((1, HD), F32)
    for b, cum in enumerate(sums):
        rows = slice(b * BLK, (b + 1) * BLK)
        for h in range(heads):
            lanes = slice(h * HD, (h + 1) * HD)
            inter = dot(query_ref[rows, lanes], enter_ref[h], ((1,), (0,)))
            weight = jnp.exp(cum[:, h : h + 1] + ahead[:, h : h + 1])
            raw_ref[rows, lanes] = local_ref[rows, lanes] + weight * inter
        ahead = ahead + cum[BLK - 1 : BLK, :]
    raw = raw_ref[...]
    ones = jnp.ones((square_ref.shape[0], raw.shape[1]), F32)
    square_ref[...] = dot(ones, raw * raw, ((1,), (1,)), lax.Precision.HIGHEST)


def norm_body(columns, raw_ref, square_ref, gate_ref, gain_ref, out_ref):
    ones = jnp.ones((square_ref.shape[0], HD), F32)
    total = dot(square_ref[...], ones, ((0,), (0,)), lax.Precision.HIGHEST)
    scale = lax.rsqrt(total / columns + EPS)
    for h in range(raw_ref.shape[1] // HD):
        lanes = slice(h * HD, (h + 1) * HD)
        gate = jax.nn.sigmoid(gate_ref[:, lanes].astype(F32))
        out_ref[:, lanes] = (raw_ref[:, lanes] * scale * gain_ref[:, lanes] * gate).astype(BF16)


def lightning(lin_query, lin_key, lin_value, lin_gate, log_decay, norm_gain, place):
    tokens, features = lin_query.shape
    heads = features // HD
    shards = lax.axis_size("seq")
    peers = lax.axis_size("head")
    logs = jnp.pad(log_decay, ((0, 0), (0, HD - heads)))
    sent = jax.ShapeDtypeStruct((heads, HD + LOG_ROWS, HD), BF16)
    send, first = call(
        states_body,
        (sent, jax.ShapeDtypeStruct((heads, HD, HD), F32)),
        (lin_key, lin_value, logs),
        flops=4 * tokens * features * HD,
        moved=4 * tokens * features,
    )
    near = [[QUAD * g + j for j in range(QUAD)] for g in range(shards // QUAD)]
    span = QUAD * QUAD
    line = [
        [span * x + QUAD * a + b for a in range(QUAD)]
        for x in range(shards // span)
        for b in range(QUAD)
    ]
    wide = [[span * x + r for x in range(shards // span)] for r in range(span)]

    def swap(array, groups):
        return lax.all_to_all(array, "seq", 0, 0, axis_index_groups=groups, tiled=True)

    mine = swap(send, near)
    local = call(
        local_body,
        jax.ShapeDtypeStruct((tokens, features), F32),
        (lin_query, lin_key, lin_value, logs, first),
        flops=4 * tokens * features * BLK,
        moved=10 * tokens * features,
    )
    small = dict(flops=10 * heads * HD * HD, moved=4 * heads * HD * HD)
    lines = swap(call(group_body, sent, (mine,), **small), line)
    wides = swap(call(group_body, sent, (lines,), **small), wide)
    entering = call(
        enter_body,
        jax.ShapeDtypeStruct((heads, HD, HD), BF16),
        (place, mine, lines, wides),
        smem=(0,),
        **small,
    )
    entering = swap(entering, near)
    raw, squares = call(
        raw_body,
        (
            jax.ShapeDtypeStruct((tokens, features), F32),
            jax.ShapeDtypeStruct((peers, tokens), F32),
        ),
        (lin_query, logs, local, entering),
        flops=2 * tokens * features * HD,
        moved=10 * tokens * features,
    )
    squares = lax.all_to_all(squares, "head", 0, 0, tiled=True)
    return call(
        functools.partial(norm_body, float(features * peers)),
        jax.ShapeDtypeStruct((tokens, features), BF16),
        (raw, squares, lin_gate, norm_gain.reshape(1, features)),
        flops=8 * tokens * features,
        moved=8 * tokens * features,
        exps=tokens * features,
    )


SCALE = math.log2(math.e) * HD ** (-0.5)


def attend_body(own, first, count, final, *refs):
    refs = list(refs)
    place_ref, docs_ref, query_ref = refs[:3]
    pieces = refs[3 : 3 + count]
    rest = refs[3 + count :]
    if own:
        before_refs, rest = None, rest
    else:
        before_refs, rest = rest[:2], rest[2:]
    if final:
        out_ref, acc_ref, max_ref = rest
    else:
        acc_ref, max_ref = rest
    tokens, features = query_ref.shape
    heads = features // HD
    blocks = tokens // MBLK
    shard = place_ref[2]
    rows = heads * MBLK
    ones = jnp.ones((tokens, HD), BF16)

    def queries(i):
        return jnp.concatenate(
            [query_ref[i * MBLK : (i + 1) * MBLK, h * HD : (h + 1) * HD] for h in range(heads)],
            axis=0,
        )

    for i in range(blocks):
        mine = docs_ref[shard * blocks + i]
        at = slice(i * rows, (i + 1) * rows)
        if not own and final:
            acc_ref[at, :] = before_refs[0][at, :]
            max_ref[at, :] = before_refs[1][at, :]
        for p in range(count):
            back = first + p
            piece = pieces[p]
            start = jnp.int32(0)
            for b in range(blocks):
                where = (shard - back) * blocks + b
                other = docs_ref[jnp.maximum(where, 0)]
                if back == 0 and b >= i:
                    continue
                start = start + jnp.where((where >= 0) & (other == mine), 0, MBLK)
            if back == 0:
                width = (i + 1) * MBLK
                scores = dot(queries(i), piece[:width, :HD], ((1,), (1,))) * SCALE
                col = lax.broadcasted_iota(jnp.int32, (rows, width), 1)
                row = lax.broadcasted_iota(jnp.int32, (rows, width), 0)
                row = (row & (MBLK - 1)) + i * MBLK
                scores = jnp.where((col <= row) & (col >= start), scores, NEG)
                top = jnp.max(scores, axis=1, keepdims=True)
                probs = jnp.exp2(scores - top).astype(BF16)
                wide = jnp.concatenate([piece[:width, HD:], ones[:width]], axis=1)
                acc_ref[at, :] = dot(probs, wide, ((1,), (0,)))
                max_ref[at, :] = jnp.broadcast_to(top, (rows, HD))
            else:

                @pl.when(start < tokens)
                def _():
                    scores = dot(queries(i), piece[:, :HD], ((1,), (1,))) * SCALE
                    col = lax.broadcasted_iota(jnp.int32, (1, tokens), 1)
                    scores = scores + jnp.where(col >= start, 0.0, NEG)
                    old = max_ref[at, :]
                    top = jnp.maximum(old, jnp.max(scores, axis=1, keepdims=True))
                    shrink = jnp.exp2(old - top)
                    probs = jnp.exp2(scores - top[:, :1]).astype(BF16)
                    wide = jnp.concatenate([piece[:, HD:], ones], axis=1)
                    added = dot(probs, wide, ((1,), (0,)))
                    acc_ref[at, :HD] = acc_ref[at, :HD] * shrink + added[:, :HD]
                    acc_ref[at, HD:] = acc_ref[at, HD:] * shrink + added[:, HD:]
                    max_ref[at, :] = top

        if final:
            done = acc_ref[at, :HD] / acc_ref[at, HD:]
            for h in range(heads):
                out_ref[i * MBLK : (i + 1) * MBLK, h * HD : (h + 1) * HD] = done[
                    h * MBLK : (h + 1) * MBLK
                ].astype(BF16)


def attend(soft_query, soft_key, soft_value, doc_ids, place):
    tokens, features = soft_query.shape
    shards = lax.axis_size("seq")
    blocks = tokens // MBLK
    hops = (DOC_MOST + blocks - 2) // blocks
    heads = features // HD
    moving = jnp.concatenate([soft_key, soft_value], axis=1)
    pieces = [moving]
    for _ in range(hops):
        moving = lax.ppermute(moving, "seq", [(s, s + 1) for s in range(shards - 1)])
        pieces.append(moving)
    carry = (
        jax.ShapeDtypeStruct((heads * tokens, 2 * HD), F32),
        jax.ShapeDtypeStruct((heads * tokens, HD), F32),
    )
    state = ()
    cuts = (0, 2, 4, 6, hops + 1)
    for lo, hi in zip(cuts[:-1], cuts[1:]):
        final = hi == hops + 1
        operands = (place, doc_ids, soft_query, *pieces[lo:hi], *state)
        aliases = None
        if state and not final:
            aliases = {len(operands) - 2: 0, len(operands) - 1: 1}
        state = call(
            functools.partial(attend_body, lo == 0, lo, hi - lo, final),
            jax.ShapeDtypeStruct((tokens, features), BF16) if final else carry,
            operands,
            smem=(0, 1),
            aliases=aliases,
            scratch=tuple(pltpu.VMEM(c.shape, c.dtype) for c in carry) if final else (),
            flops=(hi - lo) * 4 * tokens * tokens * features,
            moved=12 * tokens * features,
            exps=(hi - lo) * heads * tokens * tokens,
        )
    return state


def on_device(
    lin_query,
    lin_key,
    lin_value,
    lin_gate,
    log_decay,
    norm_gain,
    soft_query,
    soft_key,
    soft_value,
    doc_ids,
):
    shard = lax.axis_index("seq")
    span = QUAD * QUAD
    place = jnp.stack([(shard % span) // QUAD, shard // span, shard]).astype(jnp.int32)
    soft_out = attend(soft_query, soft_key, soft_value, doc_ids, place)
    lin_out = lightning(lin_query, lin_key, lin_value, lin_gate, log_decay, norm_gain, place)
    return (lin_out, soft_out)


def solution(mesh):
    spread = P("seq", "head")
    return jax.shard_map(
        on_device,
        mesh=mesh,
        in_specs=(spread,) * 5 + (P("head"),) + (spread,) * 3 + (P(),),
        out_specs=(spread, spread),
        check_vma=False,
    )
```

```python
import functools
import math

import jax
import jax.numpy as jnp
import numpy as np
from jax import lax
from jax.experimental import pallas as pl
from jax.experimental.pallas import tpu as pltpu
from jax.sharding import PartitionSpec as P

HD = 128
BLK = 256
MBLK = 128
DOC_MOST = 29
EPS = 1e-06
NEG = -1e30
LOG_FLOOR = -1000.0
LOG_ROWS = 16
QUAD = 4
F32 = jnp.float32
BF16 = jnp.bfloat16
VMEM_LIMIT = 48 * 1024 * 1024
COST = 4 * 10**9


def call(body, outs, operands, *, flops, moved, exps=0, scratch=(), smem=(), aliases=None):
    specs = [
        pl.BlockSpec(memory_space=pltpu.SMEM if i in smem else pltpu.VMEM)
        for i in range(len(operands))
    ]
    return pl.pallas_call(
        body,
        out_shape=outs,
        in_specs=specs,
        out_specs=jax.tree.map(lambda _: pl.BlockSpec(memory_space=pltpu.VMEM), outs),
        scratch_shapes=list(scratch),
        input_output_aliases=aliases or {},
        compiler_params=pltpu.CompilerParams(vmem_limit_bytes=VMEM_LIMIT),
        cost_estimate=pl.CostEstimate(
            flops=int(flops), bytes_accessed=int(moved), transcendentals=int(exps)
        ),
    )(*operands)


def dot(a, b, dims, precision=None):
    return lax.dot_general(
        a, b, (dims, ((), ())), preferred_element_type=F32, precision=precision
    )


def split(x):
    high = x.astype(BF16)
    return high, (x - high.astype(F32)).astype(BF16)


def block_sums(log_ref):
    rows = lax.broadcasted_iota(jnp.int32, (BLK, BLK), 0)
    cols = lax.broadcasted_iota(jnp.int32, (BLK, BLK), 1)
    tri = (rows >= cols).astype(F32)
    return [
        dot(tri, log_ref[b * BLK : (b + 1) * BLK, :], ((1,), (0,)), lax.Precision.HIGHEST)
        for b in range(log_ref.shape[0] // BLK)
    ]


def log_rows(total):
    first = total.astype(BF16).astype(F32)
    second = (total - first).astype(BF16).astype(F32)
    third = total - first - second
    row = lax.broadcasted_iota(jnp.int32, (LOG_ROWS, HD), 0)
    packed = jnp.where(row == 0, first, jnp.where(row == 1, second, jnp.where(row == 2, third, 0.0)))
    return packed.astype(BF16)


def states_body(key_ref, value_ref, log_ref, soft_key_ref, soft_value_ref, send_ref, first_ref, moving_ref):
    moving_ref[:, : soft_key_ref.shape[1]] = soft_key_ref[...]
    moving_ref[:, soft_key_ref.shape[1] :] = soft_value_ref[...]
    heads = key_ref.shape[1] // HD
    sums = block_sums(log_ref)
    ends = [s[BLK - 1 : BLK, :] for s in sums]
    for h in range(heads):
        lanes = slice(h * HD, (h + 1) * HD)
        state = None
        total = jnp.zeros((1, 1), F32)
        for b, cum in enumerate(sums):
            rows = slice(b * BLK, (b + 1) * BLK)
            end = ends[b][:, h : h + 1]
            weight = jnp.exp(end - cum[:, h : h + 1])
            high, low = split(key_ref[rows, lanes].astype(F32) * weight)
            value = value_ref[rows, lanes]
            local = dot(high, value, ((0,), (0,))) + dot(low, value, ((0,), (0,)))
            if b == 0:
                first_ref[h] = local
                state = local
            else:
                state = jnp.exp(end) * state + local
            total = total + end
        send_ref[h, :HD, :] = state.astype(BF16)
        total = jnp.broadcast_to(jnp.maximum(total, LOG_FLOOR), (1, HD))
        send_ref[h, HD:, :] = log_rows(total)


def local_body(query_ref, key_ref, value_ref, log_ref, first_ref, raw_ref):
    heads = key_ref.shape[1] // HD
    sums = block_sums(log_ref)
    across = [s.T for s in sums]
    rows_i = lax.broadcasted_iota(jnp.int32, (BLK, BLK), 0)
    cols_i = lax.broadcasted_iota(jnp.int32, (BLK, BLK), 1)
    causal = rows_i >= cols_i
    for b, cum in enumerate(sums):
        rows = slice(b * BLK, (b + 1) * BLK)
        for h in range(heads):
            lanes = slice(h * HD, (h + 1) * HD)
            column = cum[:, h : h + 1]
            query = query_ref[rows, lanes]
            gap = column - across[b][h : h + 1, :]
            weight = jnp.exp(jnp.where(causal, gap, NEG))
            scores = dot(query, key_ref[rows, lanes], ((1,), (1,)))
            mixed = (scores * weight).astype(BF16)
            raw = dot(mixed, value_ref[rows, lanes], ((1,), (0,)))
            if b > 0:
                high, low = split(first_ref[h])
                inter = dot(query, high, ((1,), (0,))) + dot(query, low, ((1,), (0,)))
                raw = raw + jnp.exp(column) * inter
            raw_ref[rows, lanes] = raw


def log_of(block):
    return jnp.sum(block[HD:, :].astype(F32), axis=0, keepdims=True)


def fold(parts):
    state, total = parts[0]
    for s, l in parts[1:]:
        state = jnp.exp(l) * state + s
        total = total + l
    return state, jnp.maximum(total, LOG_FLOOR)


def parts_of(got_ref):
    return [
        (got_ref[j, :HD, :].astype(F32), log_of(got_ref[j])) for j in range(got_ref.shape[0])
    ]


def group_body(got_ref, send_ref):
    state, total = fold(parts_of(got_ref))
    state = state.astype(send_ref.dtype)
    rows = log_rows(total)
    if send_ref.dtype == F32:
        row = lax.broadcasted_iota(jnp.int32, (send_ref.shape[1] - HD, HD), 0)
        rows = jnp.where(row == 0, total, 0.0)
    for j in range(send_ref.shape[0]):
        send_ref[j, :HD, :] = state
        send_ref[j, HD:, :] = rows


def before(parts, place):
    state = jnp.zeros((HD, HD), F32)
    for j, (s, l) in enumerate(parts[:-1]):
        state = jnp.where(j < place, jnp.exp(l) * state + s, state)
    return state


def log_before(parts, place):
    total = jnp.zeros((1, HD), F32)
    for j, (_, l) in enumerate(parts[:-1]):
        total = jnp.where(j < place, total + l, total)
    return total


def enter_body(place_ref, mine_ref, line_ref, wide_ref, send_ref):
    line = parts_of(line_ref)
    wide = parts_of(wide_ref)
    state = before(wide, place_ref[1])
    entering = jnp.exp(log_before(line, place_ref[0])) * state + before(line, place_ref[0])
    for j, (s, l) in enumerate(parts_of(mine_ref)):
        send_ref[j] = entering.astype(BF16)
        entering = jnp.exp(l) * entering + s


def raw_body(query_ref, log_ref, local_ref, enter_ref, raw_ref, square_ref):
    heads = query_ref.shape[1] // HD
    sums = block_sums(log_ref)
    ahead = jnp.zeros((1, HD), F32)
    for b, cum in enumerate(sums):
        rows = slice(b * BLK, (b + 1) * BLK)
        for h in range(heads):
            lanes = slice(h * HD, (h + 1) * HD)
            inter = dot(query_ref[rows, lanes], enter_ref[h], ((1,), (0,)))
            weight = jnp.exp(cum[:, h : h + 1] + ahead[:, h : h + 1])
            raw_ref[rows, lanes] = local_ref[rows, lanes] + weight * inter
        ahead = ahead + cum[BLK - 1 : BLK, :]
    raw = raw_ref[...]
    ones = jnp.ones((square_ref.shape[0], raw.shape[1]), F32)
    square_ref[...] = dot(ones, raw * raw, ((1,), (1,)), lax.Precision.HIGHEST)


def norm_body(columns, raw_ref, square_ref, gate_ref, gain_ref, out_ref):
    ones = jnp.ones((square_ref.shape[0], HD), F32)
    total = dot(square_ref[...], ones, ((0,), (0,)), lax.Precision.HIGHEST)
    scale = lax.rsqrt(total / columns + EPS)
    for h in range(raw_ref.shape[1] // HD):
        lanes = slice(h * HD, (h + 1) * HD)
        gate = jax.nn.sigmoid(gate_ref[:, lanes].astype(F32))
        out_ref[:, lanes] = (raw_ref[:, lanes] * scale * gain_ref[:, lanes] * gate).astype(BF16)


def states(lin_key, lin_value, log_decay, soft_key, soft_value):
    tokens, features = lin_key.shape
    heads = features // HD
    logs = jnp.pad(log_decay, ((0, 0), (0, HD - heads)))
    send, first, moving = call(
        states_body,
        (
            jax.ShapeDtypeStruct((heads, HD + LOG_ROWS, HD), BF16),
            jax.ShapeDtypeStruct((heads, HD, HD), F32),
            jax.ShapeDtypeStruct((tokens, 2 * soft_key.shape[1]), BF16),
        ),
        (lin_key, lin_value, logs, soft_key, soft_value),
        flops=4 * tokens * features * HD,
        moved=4 * tokens * features,
    )
    return logs, send, first, moving


def lightning(lin_query, lin_key, lin_value, lin_gate, logs, send, first, norm_gain, place):
    tokens, features = lin_query.shape
    heads = features // HD
    shards = lax.axis_size("seq")
    peers = lax.axis_size("head")
    near = [[QUAD * g + j for j in range(QUAD)] for g in range(shards // QUAD)]
    span = QUAD * QUAD
    line = [
        [span * x + QUAD * a + b for a in range(QUAD)]
        for x in range(shards // span)
        for b in range(QUAD)
    ]
    wide = [[span * x + r for x in range(shards // span)] for r in range(span)]

    def swap(array, groups):
        return lax.all_to_all(array, "seq", 0, 0, axis_index_groups=groups, tiled=True)

    mine = swap(send, near)
    local = call(
        local_body,
        jax.ShapeDtypeStruct((tokens, features), F32),
        (lin_query, lin_key, lin_value, logs, first),
        flops=4 * tokens * features * BLK,
        moved=10 * tokens * features,
    )
    small = dict(flops=10 * heads * HD * HD, moved=4 * heads * HD * HD)
    sent = jax.ShapeDtypeStruct((QUAD, HD + LOG_ROWS, HD), BF16)
    exact = jax.ShapeDtypeStruct((shards // span, HD + 8, HD), F32)
    lines = swap(call(group_body, sent, (mine,), **small), line)
    wides = swap(call(group_body, exact, (lines,), **small), wide)
    entering = call(
        enter_body,
        jax.ShapeDtypeStruct((heads, HD, HD), BF16),
        (place, mine, lines, wides),
        smem=(0,),
        **small,
    )
    entering = swap(entering, near)
    raw, squares = call(
        raw_body,
        (
            jax.ShapeDtypeStruct((tokens, features), F32),
            jax.ShapeDtypeStruct((peers, tokens), F32),
        ),
        (lin_query, logs, local, entering),
        flops=2 * tokens * features * HD,
        moved=10 * tokens * features,
    )
    squares = lax.all_to_all(squares, "head", 0, 0, tiled=True)
    return call(
        functools.partial(norm_body, float(features * peers)),
        jax.ShapeDtypeStruct((tokens, features), BF16),
        (raw, squares, lin_gate, norm_gain.reshape(1, features)),
        flops=8 * tokens * features,
        moved=8 * tokens * features,
        exps=tokens * features,
    )


SCALE = math.log2(math.e) * HD ** (-0.5)


def attend_body(backs, opening, final, *refs):
    refs = list(refs)
    place_ref, docs_ref, query_ref = refs[:3]
    pieces = refs[3 : 3 + len(backs)]
    rest = refs[3 + len(backs) :]
    tokens, features = query_ref.shape
    heads = features // HD
    blocks = tokens // MBLK
    rows = heads * MBLK
    shard = place_ref[2]
    if opening:
        acc_ref, top_ref, sum_ref = rest
    elif final:
        acc_in, top_in, sum_in, out_ref, acc_ref, top_ref, sum_ref = rest
        acc_ref[...] = acc_in[...]
        top_ref[...] = top_in[...]
        sum_ref[...] = sum_in[...]
    else:
        acc_ref, top_ref, sum_ref = rest[3:]

    for i in range(blocks):
        mine = docs_ref[shard * blocks + i]

        def queries():
            return jnp.concatenate(
                [query_ref[i * MBLK : (i + 1) * MBLK, h * HD : (h + 1) * HD] for h in range(heads)],
                axis=0,
            )

        for back, piece in zip(backs, pieces):
            start = jnp.int32(0)
            for b in range(i if back == 0 else blocks):
                where = (shard - back) * blocks + b
                other = docs_ref[jnp.maximum(where, 0)]
                start = start + jnp.where((where >= 0) & (other == mine), 0, MBLK)
            if back == 0:
                width = (i + 1) * MBLK
                scores = dot(piece[:width, :HD], queries(), ((1,), (1,)))
                key = lax.broadcasted_iota(jnp.int32, (width, rows), 0)
                token = lax.broadcasted_iota(jnp.int32, (width, rows), 1)
                token = (token & (MBLK - 1)) + i * MBLK
                scores = jnp.where((key <= token) & (key >= start), scores, NEG)
                top = jnp.max(scores, axis=0, keepdims=True)
                probs = jnp.exp2(scores * SCALE - top * SCALE)
                sum_ref[i] = jnp.sum(probs, axis=0, keepdims=True)
                acc_ref[i] = dot(piece[:width, HD:], probs.astype(BF16), ((0,), (0,)))
                top_ref[i] = top
                continue

            def add(masked):
                scores = dot(piece[:, :HD], queries(), ((1,), (1,)))
                if masked:
                    key = lax.broadcasted_iota(jnp.int32, (tokens, rows), 0)
                    scores = jnp.where(key >= start, scores, NEG)
                old = top_ref[i]
                top = jnp.maximum(old, jnp.max(scores, axis=0, keepdims=True))
                probs = jnp.exp2(scores * SCALE - top * SCALE)
                shrink = jnp.exp2((old - top) * SCALE)
                sum_ref[i] = sum_ref[i] * shrink + jnp.sum(probs, axis=0, keepdims=True)
                added = dot(piece[:, HD:], probs.astype(BF16), ((0,), (0,)))
                acc_ref[i] = acc_ref[i] * shrink + added
                top_ref[i] = top

            pl.when(start == 0)(functools.partial(add, False))
            pl.when((start > 0) & (start < tokens))(functools.partial(add, True))

        if final:
            done = (acc_ref[i] / sum_ref[i]).T
            for h in range(heads):
                out_ref[i * MBLK : (i + 1) * MBLK, h * HD : (h + 1) * HD] = done[
                    h * MBLK : (h + 1) * MBLK
                ].astype(BF16)


def forward(array, steps):
    shards = lax.axis_size("seq")
    return lax.ppermute(array, "seq", [(s, s + steps) for s in range(shards - steps)])


def attend(soft_query, own, doc_ids, place):
    tokens, features = soft_query.shape
    blocks = tokens // MBLK
    hops = (DOC_MOST + blocks - 2) // blocks
    heads = features // HD
    half = (hops + 1) // 2
    pieces = {0: own, half: forward(own, half)}
    for back in range(1, half):
        pieces[back] = forward(pieces[back - 1], 1)
    for back in range(half + 1, hops + 1):
        pieces[back] = forward(pieces[back - 1], 1)
    rows = heads * MBLK
    carry = (
        jax.ShapeDtypeStruct((blocks, HD, rows), F32),
        jax.ShapeDtypeStruct((blocks, 1, rows), F32),
        jax.ShapeDtypeStruct((blocks, 1, rows), F32),
    )
    calls = [(0,)] + [(b, b + half - 1) for b in range(1, half)]
    calls.append(tuple(range(2 * half - 1, hops + 1)))
    state = ()
    for backs in calls:
        opening, final = backs == calls[0], backs == calls[-1]
        operands = (place, doc_ids, soft_query, *(pieces[b] for b in backs), *state)
        aliases = None
        if not opening and not final:
            aliases = {len(operands) - 3 + j: j for j in range(3)}
        state = call(
            functools.partial(attend_body, backs, opening, final),
            jax.ShapeDtypeStruct((tokens, features), BF16) if final else carry,
            operands,
            smem=(0, 1),
            aliases=aliases,
            scratch=tuple(pltpu.VMEM(c.shape, c.dtype) for c in carry) if final else (),
            flops=len(backs) * COST,
            moved=12 * tokens * features,
            exps=len(backs) * heads * tokens * tokens,
        )
    return state


def on_device(
    lin_query,
    lin_key,
    lin_value,
    lin_gate,
    log_decay,
    norm_gain,
    soft_query,
    soft_key,
    soft_value,
    doc_ids,
):
    shard = lax.axis_index("seq")
    span = QUAD * QUAD
    place = jnp.stack([(shard % span) // QUAD, shard // span, shard]).astype(jnp.int32)
    logs, send, first, moving = states(lin_key, lin_value, log_decay, soft_key, soft_value)
    soft_out = attend(soft_query, moving, doc_ids, place)
    lin_out = lightning(
        lin_query, lin_key, lin_value, lin_gate, logs, send, first, norm_gain, place
    )
    return (lin_out, soft_out)


def solution(mesh):
    spread = P("seq", "head")
    return jax.shard_map(
        on_device,
        mesh=mesh,
        in_specs=(spread,) * 5 + (P("head"),) + (spread,) * 3 + (P(),),
        out_specs=(spread, spread),
        check_vma=False,
    )
```

```python
import functools
import math

import jax
import jax.numpy as jnp
import numpy as np
from jax import lax
from jax.experimental import pallas as pl
from jax.experimental.pallas import tpu as pltpu
from jax.sharding import PartitionSpec as P

HD = 128
BLK = 256
MBLK = 128
DOC_MOST = 29
EPS = 1e-06
NEG = -1e30
LOG_FLOOR = -1000.0
LOG_ROWS = 16
SAME = 8
LINE = 16
F32 = jnp.float32
BF16 = jnp.bfloat16
VMEM_LIMIT = 48 * 1024 * 1024
COST = 4 * 10**9


def call(
    body, outs, operands, *, flops, moved, exps=0, scratch=(), smem=(), aliases=None, after=()
):
    operands = (*operands, *after)
    spaces = [pltpu.SMEM if i in smem else pltpu.VMEM for i in range(len(operands) - len(after))]
    specs = [pl.BlockSpec(memory_space=m) for m in spaces + [pl.ANY] * len(after)]
    return pl.pallas_call(
        body,
        out_shape=outs,
        in_specs=specs,
        out_specs=jax.tree.map(lambda _: pl.BlockSpec(memory_space=pltpu.VMEM), outs),
        scratch_shapes=list(scratch),
        input_output_aliases=aliases or {},
        compiler_params=pltpu.CompilerParams(vmem_limit_bytes=VMEM_LIMIT),
        cost_estimate=pl.CostEstimate(
            flops=int(flops), bytes_accessed=int(moved), transcendentals=int(exps)
        ),
    )(*operands)


def dot(a, b, dims, precision=None):
    return lax.dot_general(
        a, b, (dims, ((), ())), preferred_element_type=F32, precision=precision
    )


def split(x):
    high = x.astype(BF16)
    return high, (x - high.astype(F32)).astype(BF16)


def block_sums(log_ref):
    return [dot(tri, logs, ((1,), (1,)), lax.Precision.HIGHEST) for tri, logs in blocks_of(log_ref)]


def block_sums_across(log_ref):
    return [dot(logs, tri, ((1,), (1,)), lax.Precision.HIGHEST) for tri, logs in blocks_of(log_ref)]


def blocks_of(log_ref):
    rows = lax.broadcasted_iota(jnp.int32, (BLK, BLK), 0)
    cols = lax.broadcasted_iota(jnp.int32, (BLK, BLK), 1)
    tri = (rows >= cols).astype(F32)
    return [
        (tri, log_ref[:, b * BLK : (b + 1) * BLK]) for b in range(log_ref.shape[1] // BLK)
    ]


def log_rows(total):
    first = total.astype(BF16).astype(F32)
    second = (total - first).astype(BF16).astype(F32)
    third = total - first - second
    row = lax.broadcasted_iota(jnp.int32, (LOG_ROWS, HD), 0)
    packed = jnp.where(row == 0, first, jnp.where(row == 1, second, jnp.where(row == 2, third, 0.0)))
    return packed.astype(BF16)


def states_body(key_ref, value_ref, log_ref, soft_key_ref, soft_value_ref, send_ref, first_ref, moving_ref):
    moving_ref[:, : soft_key_ref.shape[1]] = soft_key_ref[...]
    moving_ref[:, soft_key_ref.shape[1] :] = soft_value_ref[...]
    heads = key_ref.shape[1] // HD
    sums = block_sums(log_ref)
    ends = [s[BLK - 1 : BLK, :] for s in sums]
    for h in range(heads):
        lanes = slice(h * HD, (h + 1) * HD)
        state = None
        total = jnp.zeros((1, 1), F32)
        for b, cum in enumerate(sums):
            rows = slice(b * BLK, (b + 1) * BLK)
            end = ends[b][:, h : h + 1]
            weight = jnp.exp(end - cum[:, h : h + 1])
            high, low = split(key_ref[rows, lanes].astype(F32) * weight)
            value = value_ref[rows, lanes]
            local = dot(high, value, ((0,), (0,))) + dot(low, value, ((0,), (0,)))
            if b == 0:
                first_ref[h] = local
                state = local
            else:
                state = jnp.exp(end) * state + local
            total = total + end
        total = jnp.broadcast_to(jnp.maximum(total, LOG_FLOOR), (1, HD))
        share, size = send_ref.shape[0] // heads, send_ref.shape[1] - LOG_ROWS
        for j in range(share):
            send_ref[h * share + j, :size, :] = state[j * size : (j + 1) * size].astype(BF16)
            send_ref[h * share + j, size:, :] = log_rows(total)


def local_body(query_ref, key_ref, value_ref, log_ref, first_ref, raw_ref):
    heads = key_ref.shape[1] // HD
    sums = block_sums(log_ref)
    across = block_sums_across(log_ref)
    rows_i = lax.broadcasted_iota(jnp.int32, (BLK, BLK), 0)
    cols_i = lax.broadcasted_iota(jnp.int32, (BLK, BLK), 1)
    causal = rows_i >= cols_i
    for b, cum in enumerate(sums):
        rows = slice(b * BLK, (b + 1) * BLK)
        for h in range(heads):
            lanes = slice(h * HD, (h + 1) * HD)
            column = cum[:, h : h + 1]
            query = query_ref[rows, lanes]
            gap = column - across[b][h : h + 1, :]
            weight = jnp.exp(jnp.where(causal, gap, NEG))
            scores = dot(query, key_ref[rows, lanes], ((1,), (1,)))
            mixed = (scores * weight).astype(BF16)
            raw = dot(mixed, value_ref[rows, lanes], ((1,), (0,)))
            if b > 0:
                high, low = split(first_ref[h])
                inter = dot(query, high, ((1,), (0,))) + dot(query, low, ((1,), (0,)))
                raw = raw + jnp.exp(column) * inter
            raw_ref[rows, lanes] = raw


def fold(parts):
    state, total = parts[0]
    for s, l in parts[1:]:
        state = jnp.exp(l) * state + s
        total = total + l
    return state, jnp.maximum(total, LOG_FLOOR)


def parts_of(got_ref, size):
    return [
        (
            got_ref[j, :size, :].astype(F32),
            jnp.sum(got_ref[j, size:, :].astype(F32), axis=0, keepdims=True),
        )
        for j in range(got_ref.shape[0])
    ]


def line_body(got_ref, send_ref):
    size = got_ref.shape[1] - LOG_ROWS
    state, total = fold(parts_of(got_ref, size))
    row = lax.broadcasted_iota(jnp.int32, (send_ref.shape[1] - size, HD), 0)
    rows = jnp.where(row == 0, total, 0.0)
    for j in range(send_ref.shape[0]):
        send_ref[j, :size, :] = state
        send_ref[j, size:, :] = rows


def before(parts, place):
    state = jnp.zeros_like(parts[0][0])
    for j, (s, l) in enumerate(parts[:-1]):
        state = jnp.where(j < place, jnp.exp(l) * state + s, state)
    return state


def enter_body(place_ref, line_ref, wide_ref, send_ref):
    size = send_ref.shape[1]
    entering = before(parts_of(wide_ref, size), place_ref[0])
    for j, (s, l) in enumerate(parts_of(line_ref, size)):
        send_ref[j] = entering.astype(BF16)
        entering = jnp.exp(l) * entering + s


def raw_body(query_ref, log_ref, local_ref, enter_ref, raw_ref, square_ref):
    heads = query_ref.shape[1] // HD
    sums = block_sums(log_ref)
    ahead = jnp.zeros((1, heads), F32)
    for b, cum in enumerate(sums):
        rows = slice(b * BLK, (b + 1) * BLK)
        for h in range(heads):
            lanes = slice(h * HD, (h + 1) * HD)
            inter = dot(query_ref[rows, lanes], enter_ref[h], ((1,), (0,)))
            weight = jnp.exp(cum[:, h : h + 1] + ahead[:, h : h + 1])
            raw_ref[rows, lanes] = local_ref[rows, lanes] + weight * inter
        ahead = ahead + cum[BLK - 1 : BLK, :]
    raw = raw_ref[...]
    ones = jnp.ones((square_ref.shape[0], raw.shape[1]), F32)
    square_ref[...] = dot(ones, raw * raw, ((1,), (1,)), lax.Precision.HIGHEST)


def norm_body(columns, raw_ref, square_ref, gate_ref, gain_ref, out_ref):
    ones = jnp.full((square_ref.shape[0], HD), 1.0 / SAME, F32)
    total = dot(square_ref[...], ones, ((0,), (0,)), lax.Precision.HIGHEST)
    scale = lax.rsqrt(total / columns + EPS)
    for h in range(raw_ref.shape[1] // HD):
        lanes = slice(h * HD, (h + 1) * HD)
        gate = jax.nn.sigmoid(gate_ref[:, lanes].astype(F32))
        out_ref[:, lanes] = (raw_ref[:, lanes] * scale * gain_ref[:, lanes] * gate).astype(BF16)


def states(lin_key, lin_value, log_decay, soft_key, soft_value):
    tokens, features = lin_key.shape
    heads = features // HD
    logs = log_decay.T
    send, first, moving = call(
        states_body,
        (
            jax.ShapeDtypeStruct((LINE, heads * HD // LINE + LOG_ROWS, HD), BF16),
            jax.ShapeDtypeStruct((heads, HD, HD), F32),
            jax.ShapeDtypeStruct((tokens, 2 * soft_key.shape[1]), BF16),
        ),
        (lin_key, lin_value, logs, soft_key, soft_value),
        flops=4 * tokens * features * HD,
        moved=4 * tokens * features,
    )
    return logs, send, first, moving


def lightning_local(lin_query, lin_key, lin_value, logs, send, first):
    tokens, features = lin_query.shape
    heads = features // HD
    shards = lax.axis_size("seq")
    peers = lax.axis_size("head")
    line = [[LINE * x + z for z in range(LINE)] for x in range(shards // LINE)]
    wide = [[LINE * x + z for x in range(shards // LINE)] for z in range(LINE)]

    def swap(array, groups):
        return lax.all_to_all(array, "seq", 0, 0, axis_index_groups=groups, tiled=True)

    lines = swap(send, line)
    local = call(
        local_body,
        jax.ShapeDtypeStruct((tokens, features), F32),
        (lin_query, lin_key, lin_value, logs, first),
        flops=4 * tokens * features * BLK,
        moved=10 * tokens * features,
    )
    small = dict(flops=10 * heads * HD * HD, moved=4 * heads * HD * HD)
    size = heads * HD // LINE
    total = jax.ShapeDtypeStruct((shards // LINE, size + 8, HD), F32)
    total = call(line_body, total, (lines,), **small)
    return local, lines, total, swap, line, wide, small


def lightning(lin_query, lin_gate, logs, norm_gain, place, local, lines, total, swap, line, wide, small):
    tokens, features = lin_query.shape
    heads = features // HD
    peers = lax.axis_size("head")
    size = heads * HD // LINE
    wides = swap(total, wide)
    entering = call(
        enter_body,
        jax.ShapeDtypeStruct((LINE, size, HD), BF16),
        (place, lines, wides),
        smem=(0,),
        **small,
    )
    entering = swap(entering, line).reshape(heads, HD, HD)
    raw, squares = call(
        raw_body,
        (
            jax.ShapeDtypeStruct((tokens, features), F32),
            jax.ShapeDtypeStruct((peers * SAME, tokens), F32),
        ),
        (lin_query, logs, local, entering),
        flops=2 * tokens * features * HD,
        moved=10 * tokens * features,
    )
    squares = lax.all_to_all(squares, "head", 0, 0, tiled=True)
    return call(
        functools.partial(norm_body, float(features * peers)),
        jax.ShapeDtypeStruct((tokens, features), BF16),
        (raw, squares, lin_gate, norm_gain.reshape(1, features)),
        flops=8 * tokens * features,
        moved=8 * tokens * features,
        exps=tokens * features,
    )


SCALE = math.log2(math.e) * HD ** (-0.5)


def attend_body(backs, opening, final, *refs):
    place_ref, docs_ref, query_ref, piece_ref = refs[:4]
    pieces = [
        piece_ref.at[:, 2 * HD * j : 2 * HD * (j + 1)] for j in range(piece_ref.shape[1] // (2 * HD))
    ]
    rest = refs[4:]
    tokens, features = query_ref.shape
    heads = features // HD
    blocks = tokens // MBLK
    rows = heads * MBLK
    shard = place_ref[1]
    if opening:
        acc_ref, top_ref, sum_ref = rest
    elif final:
        acc_in, top_in, sum_in, out_ref, acc_ref, top_ref, sum_ref = rest
        acc_ref[...] = acc_in[...]
        top_ref[...] = top_in[...]
        sum_ref[...] = sum_in[...]
    else:
        acc_ref, top_ref, sum_ref = rest[3:]

    for i in range(blocks):
        mine = docs_ref[shard * blocks + i]

        def queries():
            return jnp.concatenate(
                [query_ref[i * MBLK : (i + 1) * MBLK, h * HD : (h + 1) * HD] for h in range(heads)],
                axis=0,
            )

        for back, piece in zip(backs, pieces):
            start = jnp.int32(0)
            for b in range(i if back == 0 else blocks):
                where = (shard - back) * blocks + b
                other = docs_ref[jnp.maximum(where, 0)]
                start = start + jnp.where((where >= 0) & (other == mine), 0, MBLK)
            if back == 0:
                width = (i + 1) * MBLK
                scores = dot(piece[:width, :HD], queries(), ((1,), (1,)))
                key = lax.broadcasted_iota(jnp.int32, (width, rows), 0)
                token = lax.broadcasted_iota(jnp.int32, (width, rows), 1)
                token = (token & (MBLK - 1)) + i * MBLK
                scores = jnp.where((key <= token) & (key >= start), scores, NEG)
                top = jnp.max(scores, axis=0, keepdims=True)
                probs = jnp.exp2(scores * SCALE - top * SCALE)
                sum_ref[i] = jnp.sum(probs, axis=0, keepdims=True)
                acc_ref[i] = dot(piece[:width, HD:], probs.astype(BF16), ((0,), (0,)))
                top_ref[i] = top
                continue

            def add(masked):
                scores = dot(piece[:, :HD], queries(), ((1,), (1,)))
                if masked:
                    key = lax.broadcasted_iota(jnp.int32, (tokens, rows), 0)
                    scores = jnp.where(key >= start, scores, NEG)
                old = top_ref[i]
                top = jnp.maximum(old, jnp.max(scores, axis=0, keepdims=True))
                probs = jnp.exp2(scores * SCALE - top * SCALE)
                shrink = jnp.exp2((old - top) * SCALE)
                sum_ref[i] = sum_ref[i] * shrink + jnp.sum(probs, axis=0, keepdims=True)
                added = dot(piece[:, HD:], probs.astype(BF16), ((0,), (0,)))
                acc_ref[i] = acc_ref[i] * shrink + added
                top_ref[i] = top

            pl.when(start == 0)(functools.partial(add, False))
            pl.when((start > 0) & (start < tokens))(functools.partial(add, True))

        if final:
            done = (acc_ref[i] / sum_ref[i]).T
            for h in range(heads):
                out_ref[i * MBLK : (i + 1) * MBLK, h * HD : (h + 1) * HD] = done[
                    h * MBLK : (h + 1) * MBLK
                ].astype(BF16)


def join_body(first_ref, second_ref, *rest):
    both_ref = rest[-1]
    both_ref[:, : first_ref.shape[1]] = first_ref[...]
    both_ref[:, first_ref.shape[1] :] = second_ref[...]


def forward(array, steps):
    shards = lax.axis_size("seq")
    return lax.ppermute(array, "seq", [(s, s + steps) for s in range(shards - steps)])


def attend(soft_query, own, doc_ids, place, after):
    tokens, features = soft_query.shape
    blocks = tokens // MBLK
    hops = (DOC_MOST + blocks - 2) // blocks
    heads = features // HD
    half = (hops + 1) // 2
    rows = heads * MBLK
    carry = (
        jax.ShapeDtypeStruct((blocks, HD, rows), F32),
        jax.ShapeDtypeStruct((blocks, 1, rows), F32),
        jax.ShapeDtypeStruct((blocks, 1, rows), F32),
    )

    def absorb(state, backs, array, final=False):
        operands = (place, doc_ids, soft_query, array, *state)
        aliases = {len(operands) - 3 + j: j for j in range(3)}
        return call(
            functools.partial(attend_body, backs, not state, final),
            jax.ShapeDtypeStruct((tokens, features), BF16) if final else carry,
            operands,
            smem=(0, 1),
            aliases=aliases if state and not final else None,
            scratch=tuple(pltpu.VMEM(c.shape, c.dtype) for c in carry) if final else (),
            flops=len(backs) * COST,
            moved=12 * tokens * features,
            exps=len(backs) * heads * tokens * tokens,
        )

    far = forward(own, half)
    state = absorb((), (0,), own)
    moving = call(
        join_body,
        jax.ShapeDtypeStruct((tokens, 2 * own.shape[1]), BF16),
        (own, far),
        flops=0,
        moved=4 * own.size,
        after=(state[1], *after),
    )
    state = absorb(state, (half,), far)
    for back in range(1, half):
        moving = forward(moving, 1)
        state = absorb(state, (back, back + half), moving, back == half - 1)
    return state


def on_device(
    lin_query,
    lin_key,
    lin_value,
    lin_gate,
    log_decay,
    norm_gain,
    soft_query,
    soft_key,
    soft_value,
    doc_ids,
):
    shard = lax.axis_index("seq")
    place = jnp.stack([shard // LINE, shard]).astype(jnp.int32)
    logs, send, first, moving = states(lin_key, lin_value, log_decay, soft_key, soft_value)
    parts = lightning_local(lin_query, lin_key, lin_value, logs, send, first)
    soft_out = attend(soft_query, moving, doc_ids, place, (parts[0], parts[2]))
    lin_out = lightning(lin_query, lin_gate, logs, norm_gain, place, *parts)
    return (lin_out, soft_out)


def solution(mesh):
    spread = P("seq", "head")
    return jax.shard_map(
        on_device,
        mesh=mesh,
        in_specs=(spread,) * 5 + (P("head"),) + (spread,) * 3 + (P(),),
        out_specs=(spread, spread),
        check_vma=False,
    )
```

```python
import functools
import math

import jax
import jax.numpy as jnp
import numpy as np
from jax import lax
from jax.experimental import pallas as pl
from jax.experimental.pallas import tpu as pltpu
from jax.sharding import PartitionSpec as P

HD = 128
BLK = 256
MBLK = 128
DOC_MOST = 29
EPS = 1e-06
NEG = -1e30
LOG_FLOOR = -1000.0
LOG_ROWS = 16
SAME = 8
QUAD = 4
F32 = jnp.float32
BF16 = jnp.bfloat16
VMEM_LIMIT = 48 * 1024 * 1024
COST = 4 * 10**9


def call(
    body, outs, operands, *, flops, moved, exps=0, scratch=(), smem=(), aliases=None, after=()
):
    count = len(operands)
    if after:
        inner = body
        body = lambda *refs: inner(*refs[:count], *refs[count + len(after) :])
    operands = (*operands, *after)
    spaces = [pltpu.SMEM if i in smem else pltpu.VMEM for i in range(len(operands) - len(after))]
    specs = [pl.BlockSpec(memory_space=m) for m in spaces + [pl.ANY] * len(after)]
    return pl.pallas_call(
        body,
        out_shape=outs,
        in_specs=specs,
        out_specs=jax.tree.map(lambda _: pl.BlockSpec(memory_space=pltpu.VMEM), outs),
        scratch_shapes=list(scratch),
        input_output_aliases=aliases or {},
        compiler_params=pltpu.CompilerParams(vmem_limit_bytes=VMEM_LIMIT),
        cost_estimate=pl.CostEstimate(
            flops=int(flops), bytes_accessed=int(moved), transcendentals=int(exps)
        ),
    )(*operands)


def dot(a, b, dims, precision=None):
    return lax.dot_general(
        a, b, (dims, ((), ())), preferred_element_type=F32, precision=precision
    )


def split(x):
    high = x.astype(BF16)
    return high, (x - high.astype(F32)).astype(BF16)


def block_sums(log_ref):
    return [dot(tri, logs, ((1,), (1,)), lax.Precision.HIGHEST) for tri, logs in blocks_of(log_ref)]


def block_sums_across(log_ref):
    return [dot(logs, tri, ((1,), (1,)), lax.Precision.HIGHEST) for tri, logs in blocks_of(log_ref)]


def blocks_of(log_ref):
    rows = lax.broadcasted_iota(jnp.int32, (BLK, BLK), 0)
    cols = lax.broadcasted_iota(jnp.int32, (BLK, BLK), 1)
    tri = (rows >= cols).astype(F32)
    return [
        (tri, log_ref[:, b * BLK : (b + 1) * BLK]) for b in range(log_ref.shape[1] // BLK)
    ]


def log_rows(total):
    first = total.astype(BF16).astype(F32)
    second = (total - first).astype(BF16).astype(F32)
    third = total - first - second
    row = lax.broadcasted_iota(jnp.int32, (LOG_ROWS, HD), 0)
    packed = jnp.where(row == 0, first, jnp.where(row == 1, second, jnp.where(row == 2, third, 0.0)))
    return packed.astype(BF16)


def states_body(key_ref, value_ref, log_ref, soft_key_ref, soft_value_ref, send_ref, first_ref, moving_ref):
    moving_ref[:, : soft_key_ref.shape[1]] = soft_key_ref[...]
    moving_ref[:, soft_key_ref.shape[1] :] = soft_value_ref[...]
    heads = key_ref.shape[1] // HD
    sums = block_sums(log_ref)
    ends = [s[BLK - 1 : BLK, :] for s in sums]
    for h in range(heads):
        lanes = slice(h * HD, (h + 1) * HD)
        state = None
        total = jnp.zeros((1, 1), F32)
        for b, cum in enumerate(sums):
            rows = slice(b * BLK, (b + 1) * BLK)
            end = ends[b][:, h : h + 1]
            weight = jnp.exp(end - cum[:, h : h + 1])
            high, low = split(key_ref[rows, lanes].astype(F32) * weight)
            value = value_ref[rows, lanes]
            local = dot(high, value, ((0,), (0,))) + dot(low, value, ((0,), (0,)))
            if b == 0:
                first_ref[h] = local
                state = local
            else:
                state = jnp.exp(end) * state + local
            total = total + end
        total = jnp.broadcast_to(jnp.maximum(total, LOG_FLOOR), (1, HD))
        share, size = send_ref.shape[0] // heads, send_ref.shape[1] - LOG_ROWS
        for j in range(share):
            send_ref[h * share + j, :size, :] = state[j * size : (j + 1) * size].astype(BF16)
            send_ref[h * share + j, size:, :] = log_rows(total)


def local_body(query_ref, key_ref, value_ref, log_ref, first_ref, raw_ref):
    heads = key_ref.shape[1] // HD
    sums = block_sums(log_ref)
    across = block_sums_across(log_ref)
    rows_i = lax.broadcasted_iota(jnp.int32, (BLK, BLK), 0)
    cols_i = lax.broadcasted_iota(jnp.int32, (BLK, BLK), 1)
    causal = rows_i >= cols_i
    for b, cum in enumerate(sums):
        rows = slice(b * BLK, (b + 1) * BLK)
        for h in range(heads):
            lanes = slice(h * HD, (h + 1) * HD)
            column = cum[:, h : h + 1]
            query = query_ref[rows, lanes]
            gap = column - across[b][h : h + 1, :]
            weight = jnp.exp(jnp.where(causal, gap, NEG))
            scores = dot(query, key_ref[rows, lanes], ((1,), (1,)))
            mixed = (scores * weight).astype(BF16)
            raw = dot(mixed, value_ref[rows, lanes], ((1,), (0,)))
            if b > 0:
                high, low = split(first_ref[h])
                inter = dot(query, high, ((1,), (0,))) + dot(query, low, ((1,), (0,)))
                raw = raw + jnp.exp(column) * inter
            raw_ref[rows, lanes] = raw


def fold(parts):
    state, total = parts[0]
    for s, l in parts[1:]:
        state = jnp.exp(l) * state + s
        total = total + l
    return state, jnp.maximum(total, LOG_FLOOR)


def parts_of(got_ref, size):
    return [
        (
            got_ref[j, :size, :].astype(F32),
            jnp.sum(got_ref[j, size:, :].astype(F32), axis=0, keepdims=True),
        )
        for j in range(got_ref.shape[0])
    ]


def group_body(got_ref, send_ref):
    size = got_ref.shape[1] - LOG_ROWS
    state, total = fold(parts_of(got_ref, size))
    state = state.astype(send_ref.dtype)
    if send_ref.dtype == F32:
        row = lax.broadcasted_iota(jnp.int32, (send_ref.shape[1] - size, HD), 0)
        rows = jnp.where(row == 0, total, 0.0)
    else:
        rows = log_rows(total)
    for j in range(send_ref.shape[0]):
        send_ref[j, :size, :] = state
        send_ref[j, size:, :] = rows


def before(parts, place):
    state = jnp.zeros_like(parts[0][0])
    for j, (s, l) in enumerate(parts[:-1]):
        state = jnp.where(j < place, jnp.exp(l) * state + s, state)
    return state


def log_before(parts, place):
    total = jnp.zeros_like(parts[0][1])
    for j, (_, l) in enumerate(parts[:-1]):
        total = jnp.where(j < place, total + l, total)
    return total


def enter_body(place_ref, mine_ref, line_ref, wide_ref, send_ref):
    size = send_ref.shape[1]
    line = parts_of(line_ref, size)
    state = before(parts_of(wide_ref, size), place_ref[0])
    entering = jnp.exp(log_before(line, place_ref[2])) * state + before(line, place_ref[2])
    for j, (s, l) in enumerate(parts_of(mine_ref, size)):
        send_ref[j] = entering.astype(BF16)
        entering = jnp.exp(l) * entering + s


def raw_body(query_ref, log_ref, local_ref, enter_ref, raw_ref, square_ref):
    heads = query_ref.shape[1] // HD
    sums = block_sums(log_ref)
    ahead = jnp.zeros((1, heads), F32)
    for b, cum in enumerate(sums):
        rows = slice(b * BLK, (b + 1) * BLK)
        for h in range(heads):
            lanes = slice(h * HD, (h + 1) * HD)
            inter = dot(query_ref[rows, lanes], enter_ref[h], ((1,), (0,)))
            weight = jnp.exp(cum[:, h : h + 1] + ahead[:, h : h + 1])
            raw_ref[rows, lanes] = local_ref[rows, lanes] + weight * inter
        ahead = ahead + cum[BLK - 1 : BLK, :]
    raw = raw_ref[...]
    ones = jnp.ones((square_ref.shape[0], raw.shape[1]), F32)
    square_ref[...] = dot(ones, raw * raw, ((1,), (1,)), lax.Precision.HIGHEST)


def norm_body(columns, raw_ref, square_ref, gate_ref, gain_ref, out_ref):
    ones = jnp.full((square_ref.shape[0], HD), 1.0 / SAME, F32)
    total = dot(square_ref[...], ones, ((0,), (0,)), lax.Precision.HIGHEST)
    scale = lax.rsqrt(total / columns + EPS)
    for h in range(raw_ref.shape[1] // HD):
        lanes = slice(h * HD, (h + 1) * HD)
        gate = jax.nn.sigmoid(gate_ref[:, lanes].astype(F32))
        out_ref[:, lanes] = (raw_ref[:, lanes] * scale * gain_ref[:, lanes] * gate).astype(BF16)


def states(lin_key, lin_value, log_decay, soft_key, soft_value):
    tokens, features = lin_key.shape
    heads = features // HD
    logs = log_decay.T
    send, first, moving = call(
        states_body,
        (
            jax.ShapeDtypeStruct((QUAD, heads * HD // QUAD + LOG_ROWS, HD), BF16),
            jax.ShapeDtypeStruct((heads, HD, HD), F32),
            jax.ShapeDtypeStruct((tokens, 2 * soft_key.shape[1]), BF16),
        ),
        (lin_key, lin_value, logs, soft_key, soft_value),
        flops=4 * tokens * features * HD,
        moved=4 * tokens * features,
    )
    return logs, send, first, moving


def swap(array, groups):
    return lax.all_to_all(array, "seq", 0, 0, axis_index_groups=groups, tiled=True)


def gate_body(*refs):
    pass


def gate(array, *after):
    anywhere = pl.BlockSpec(memory_space=pl.ANY)
    return pl.pallas_call(
        gate_body,
        out_shape=jax.ShapeDtypeStruct(array.shape, array.dtype),
        in_specs=[anywhere] * (1 + len(after)),
        out_specs=anywhere,
        input_output_aliases={0: 0},
        cost_estimate=pl.CostEstimate(flops=0, bytes_accessed=0, transcendentals=0),
    )(array, *after)


SCALE = math.log2(math.e) * HD ** (-0.5)


def attend_body(backs, opening, final, *refs):
    place_ref, docs_ref, query_ref = refs[:3]
    pieces = refs[3 : 3 + len(backs)]
    rest = refs[3 + len(backs) :]
    tokens, features = query_ref.shape
    heads = features // HD
    blocks = tokens // MBLK
    rows = heads * MBLK
    shard = place_ref[1]
    if opening:
        acc_ref, top_ref, sum_ref = rest
    elif final:
        acc_in, top_in, sum_in, out_ref, acc_ref, top_ref, sum_ref = rest
        acc_ref[...] = acc_in[...]
        top_ref[...] = top_in[...]
        sum_ref[...] = sum_in[...]
    else:
        acc_ref, top_ref, sum_ref = rest[3:]

    for i in range(blocks):
        mine = docs_ref[shard * blocks + i]

        def queries():
            return jnp.concatenate(
                [query_ref[i * MBLK : (i + 1) * MBLK, h * HD : (h + 1) * HD] for h in range(heads)],
                axis=0,
            )

        for back, piece in zip(backs, pieces):
            start = jnp.int32(0)
            for b in range(i if back == 0 else blocks):
                where = (shard - back) * blocks + b
                other = docs_ref[jnp.maximum(where, 0)]
                start = start + jnp.where((where >= 0) & (other == mine), 0, MBLK)
            if back == 0:
                width = (i + 1) * MBLK
                scores = dot(piece[:width, :HD], queries(), ((1,), (1,)))
                key = lax.broadcasted_iota(jnp.int32, (width, rows), 0)
                token = lax.broadcasted_iota(jnp.int32, (width, rows), 1)
                token = (token & (MBLK - 1)) + i * MBLK
                scores = jnp.where((key <= token) & (key >= start), scores, NEG)
                top = jnp.max(scores, axis=0, keepdims=True)
                probs = jnp.exp2(scores * SCALE - top * SCALE)
                sum_ref[i] = jnp.sum(probs, axis=0, keepdims=True)
                acc_ref[i] = dot(piece[:width, HD:], probs.astype(BF16), ((0,), (0,)))
                top_ref[i] = top
                continue

            def add(masked):
                scores = dot(piece[:, :HD], queries(), ((1,), (1,)))
                if masked:
                    key = lax.broadcasted_iota(jnp.int32, (tokens, rows), 0)
                    scores = jnp.where(key >= start, scores, NEG)
                old = top_ref[i]
                top = jnp.maximum(old, jnp.max(scores, axis=0, keepdims=True))
                probs = jnp.exp2(scores * SCALE - top * SCALE)
                shrink = jnp.exp2((old - top) * SCALE)
                sum_ref[i] = sum_ref[i] * shrink + jnp.sum(probs, axis=0, keepdims=True)
                added = dot(piece[:, HD:], probs.astype(BF16), ((0,), (0,)))
                acc_ref[i] = acc_ref[i] * shrink + added
                top_ref[i] = top

            pl.when(start == 0)(functools.partial(add, False))
            pl.when((start > 0) & (start < tokens))(functools.partial(add, True))

        if final:
            done = (acc_ref[i] / sum_ref[i]).T
            for h in range(heads):
                out_ref[i * MBLK : (i + 1) * MBLK, h * HD : (h + 1) * HD] = done[
                    h * MBLK : (h + 1) * MBLK
                ].astype(BF16)


def forward(array, steps):
    shards = lax.axis_size("seq")
    return lax.ppermute(array, "seq", [(s, s + steps) for s in range(shards - steps)])


def absorber(soft_query, doc_ids, place):
    tokens, features = soft_query.shape
    blocks = tokens // MBLK
    heads = features // HD
    rows = heads * MBLK
    carry = (
        jax.ShapeDtypeStruct((blocks, HD, rows), F32),
        jax.ShapeDtypeStruct((blocks, 1, rows), F32),
        jax.ShapeDtypeStruct((blocks, 1, rows), F32),
    )

    def absorb(state, backs, arrays, final=False):
        operands = (place, doc_ids, soft_query, *arrays, *state)
        aliases = {len(operands) - 3 + j: j for j in range(3)}
        return call(
            functools.partial(attend_body, backs, not state, final),
            jax.ShapeDtypeStruct((tokens, features), BF16) if final else carry,
            operands,
            smem=(0, 1),
            aliases=aliases if state and not final else None,
            scratch=tuple(pltpu.VMEM(c.shape, c.dtype) for c in carry) if final else (),
            flops=len(backs) * COST,
            moved=12 * tokens * features,
            exps=len(backs) * heads * tokens * tokens,
        )

    return absorb


def on_device(
    lin_query,
    lin_key,
    lin_value,
    lin_gate,
    log_decay,
    norm_gain,
    soft_query,
    soft_key,
    soft_value,
    doc_ids,
):
    tokens, features = lin_query.shape
    heads = features // HD
    shards = lax.axis_size("seq")
    peers = lax.axis_size("head")
    shard = lax.axis_index("seq")
    span = QUAD * QUAD
    place = jnp.stack([shard // span, shard, (shard % span) // QUAD]).astype(jnp.int32)
    near = [[QUAD * g + j for j in range(QUAD)] for g in range(shards // QUAD)]
    line = [
        [span * x + QUAD * a + b for a in range(QUAD)]
        for x in range(shards // span)
        for b in range(QUAD)
    ]
    wide = [[span * x + r for x in range(shards // span)] for r in range(span)]
    size = heads * HD // QUAD
    small = dict(flops=10 * heads * HD * HD, moved=4 * heads * HD * HD)
    hops = (DOC_MOST + tokens // MBLK - 2) // (tokens // MBLK)
    absorb = absorber(soft_query, doc_ids, place)

    logs, send, first, own = states(lin_key, lin_value, log_decay, soft_key, soft_value)
    mine = swap(send, near)
    back = [own]

    def hop(*after):
        if after:
            back[-1] = gate(back[-1], *after)
        back.append(forward(back[-1], 1))

    hop()
    local = call(
        local_body,
        jax.ShapeDtypeStruct((tokens, features), F32),
        (lin_query, lin_key, lin_value, logs, first),
        flops=4 * tokens * features * BLK,
        moved=10 * tokens * features,
    )
    state = absorb((), (0,), back[:1])
    hop(local, state[1])
    group = call(
        group_body,
        jax.ShapeDtypeStruct((QUAD, size + LOG_ROWS, HD), BF16),
        (mine,),
        **small,
    )
    lines = swap(group, line)
    hop(group)
    state = absorb(state, (1, 2), back[1:3])
    hop(state[1])
    total = call(
        group_body,
        jax.ShapeDtypeStruct((shards // span, size + 8, HD), F32),
        (lines,),
        **small,
    )
    wides = swap(total, wide)
    hop(total)
    state = absorb(state, (3, 4), back[3:5])
    hop(state[1])
    entering = call(
        enter_body,
        jax.ShapeDtypeStruct((QUAD, size, HD), BF16),
        (place, mine, lines, wides),
        smem=(0,),
        **small,
    )
    hop(entering)
    entering = swap(entering, near).reshape(heads, HD, HD)
    state = absorb(state, (5, 6), back[5:7])
    raw, squares = call(
        raw_body,
        (
            jax.ShapeDtypeStruct((tokens, features), F32),
            jax.ShapeDtypeStruct((peers * SAME, tokens), F32),
        ),
        (lin_query, logs, local, entering),
        flops=2 * tokens * features * HD,
        moved=10 * tokens * features,
    )
    squares = lax.all_to_all(squares, "head", 0, 0, tiled=True)
    lin_out = call(
        functools.partial(norm_body, float(features * peers)),
        jax.ShapeDtypeStruct((tokens, features), BF16),
        (raw, squares, lin_gate, norm_gain.reshape(1, features)),
        flops=8 * tokens * features,
        moved=8 * tokens * features,
        exps=tokens * features,
    )
    assert len(back) == hops + 1
    soft_out = absorb(state, tuple(range(7, hops + 1)), back[7:], True)
    return (lin_out, soft_out)


def solution(mesh):
    spread = P("seq", "head")
    return jax.shard_map(
        on_device,
        mesh=mesh,
        in_specs=(spread,) * 5 + (P("head"),) + (spread,) * 3 + (P(),),
        out_specs=(spread, spread),
        check_vma=False,
    )
```

```python
import functools
import math

import jax
import jax.numpy as jnp
import numpy as np
from jax import lax
from jax.experimental import pallas as pl
from jax.experimental.pallas import tpu as pltpu
from jax.sharding import PartitionSpec as P

HD = 128
BLK = 256
MBLK = 128
DOC_MOST = 29
EPS = 1e-06
NEG = -1e30
LOG_FLOOR = -1000.0
LOG_ROWS = 16
SAME = 8
QUAD = 4
F32 = jnp.float32
BF16 = jnp.bfloat16
VMEM_LIMIT = 8 * 1024 * 1024
COST = 4 * 10**9


def call(
    body, outs, operands, *, flops, moved, exps=0, scratch=(), smem=(), aliases=None, after=()
):
    count = len(operands)
    if after:
        inner = body
        body = lambda *refs: inner(*refs[:count], *refs[count + len(after) :])
    operands = (*operands, *after)
    spaces = [pltpu.SMEM if i in smem else pltpu.VMEM for i in range(len(operands) - len(after))]
    specs = [pl.BlockSpec(memory_space=m) for m in spaces + [pl.ANY] * len(after)]
    return pl.pallas_call(
        body,
        out_shape=outs,
        in_specs=specs,
        out_specs=jax.tree.map(lambda _: pl.BlockSpec(memory_space=pltpu.VMEM), outs),
        scratch_shapes=list(scratch),
        input_output_aliases=aliases or {},
        compiler_params=pltpu.CompilerParams(vmem_limit_bytes=VMEM_LIMIT),
        cost_estimate=pl.CostEstimate(
            flops=int(flops), bytes_accessed=int(moved), transcendentals=int(exps)
        ),
    )(*operands)


def dot(a, b, dims, precision=None):
    return lax.dot_general(
        a, b, (dims, ((), ())), preferred_element_type=F32, precision=precision
    )


def split(x):
    high = x.astype(BF16)
    return high, (x - high.astype(F32)).astype(BF16)


def block_sums(log_ref):
    return [dot(tri, logs, ((1,), (1,)), lax.Precision.HIGHEST) for tri, logs in blocks_of(log_ref)]


def block_sums_across(log_ref):
    return [dot(logs, tri, ((1,), (1,)), lax.Precision.HIGHEST) for tri, logs in blocks_of(log_ref)]


def blocks_of(log_ref):
    rows = lax.broadcasted_iota(jnp.int32, (BLK, BLK), 0)
    cols = lax.broadcasted_iota(jnp.int32, (BLK, BLK), 1)
    tri = (rows >= cols).astype(F32)
    return [
        (tri, log_ref[:, b * BLK : (b + 1) * BLK]) for b in range(log_ref.shape[1] // BLK)
    ]


def log_rows(total):
    first = total.astype(BF16).astype(F32)
    second = (total - first).astype(BF16).astype(F32)
    third = total - first - second
    row = lax.broadcasted_iota(jnp.int32, (LOG_ROWS, HD), 0)
    packed = jnp.where(row == 0, first, jnp.where(row == 1, second, jnp.where(row == 2, third, 0.0)))
    return packed.astype(BF16)


def states_body(key_ref, value_ref, log_ref, soft_key_ref, soft_value_ref, send_ref, first_ref, moving_ref):
    moving_ref[:, : soft_key_ref.shape[1]] = soft_key_ref[...]
    moving_ref[:, soft_key_ref.shape[1] :] = soft_value_ref[...]
    heads = key_ref.shape[1] // HD
    sums = block_sums(log_ref)
    ends = [s[BLK - 1 : BLK, :] for s in sums]
    for h in range(heads):
        lanes = slice(h * HD, (h + 1) * HD)
        state = None
        total = jnp.zeros((1, 1), F32)
        for b, cum in enumerate(sums):
            rows = slice(b * BLK, (b + 1) * BLK)
            end = ends[b][:, h : h + 1]
            weight = jnp.exp(end - cum[:, h : h + 1])
            high, low = split(key_ref[rows, lanes].astype(F32) * weight)
            value = value_ref[rows, lanes]
            local = dot(high, value, ((0,), (0,))) + dot(low, value, ((0,), (0,)))
            if b == 0:
                first_ref[h] = local
                state = local
            else:
                state = jnp.exp(end) * state + local
            total = total + end
        total = jnp.broadcast_to(jnp.maximum(total, LOG_FLOOR), (1, HD))
        share, size = send_ref.shape[0] // heads, send_ref.shape[1] - LOG_ROWS
        for j in range(share):
            send_ref[h * share + j, :size, :] = state[j * size : (j + 1) * size].astype(BF16)
            send_ref[h * share + j, size:, :] = log_rows(total)


def local_body(query_ref, key_ref, value_ref, log_ref, first_ref, raw_ref):
    heads = key_ref.shape[1] // HD
    sums = block_sums(log_ref)
    across = block_sums_across(log_ref)
    rows_i = lax.broadcasted_iota(jnp.int32, (BLK, BLK), 0)
    cols_i = lax.broadcasted_iota(jnp.int32, (BLK, BLK), 1)
    causal = rows_i >= cols_i
    for b, cum in enumerate(sums):
        rows = slice(b * BLK, (b + 1) * BLK)
        for h in range(heads):
            lanes = slice(h * HD, (h + 1) * HD)
            column = cum[:, h : h + 1]
            query = query_ref[rows, lanes]
            gap = column - across[b][h : h + 1, :]
            weight = jnp.exp(jnp.where(causal, gap, NEG))
            scores = dot(query, key_ref[rows, lanes], ((1,), (1,)))
            mixed = (scores * weight).astype(BF16)
            raw = dot(mixed, value_ref[rows, lanes], ((1,), (0,)))
            if b > 0:
                high, low = split(first_ref[h])
                inter = dot(query, high, ((1,), (0,))) + dot(query, low, ((1,), (0,)))
                raw = raw + jnp.exp(column) * inter
            raw_ref[rows, lanes] = raw


def fold(parts):
    state, total = parts[0]
    for s, l in parts[1:]:
        state = jnp.exp(l) * state + s
        total = total + l
    return state, jnp.maximum(total, LOG_FLOOR)


def parts_of(got_ref, size):
    return [
        (
            got_ref[j, :size, :].astype(F32),
            jnp.sum(got_ref[j, size:, :].astype(F32), axis=0, keepdims=True),
        )
        for j in range(got_ref.shape[0])
    ]


def group_body(got_ref, send_ref):
    size = got_ref.shape[1] - LOG_ROWS
    state, total = fold(parts_of(got_ref, size))
    state = state.astype(send_ref.dtype)
    if send_ref.dtype == F32:
        row = lax.broadcasted_iota(jnp.int32, (send_ref.shape[1] - size, HD), 0)
        rows = jnp.where(row == 0, total, 0.0)
    else:
        rows = log_rows(total)
    for j in range(send_ref.shape[0]):
        send_ref[j, :size, :] = state
        send_ref[j, size:, :] = rows


def before(parts, place):
    state = jnp.zeros_like(parts[0][0])
    for j, (s, l) in enumerate(parts[:-1]):
        state = jnp.where(j < place, jnp.exp(l) * state + s, state)
    return state


def log_before(parts, place):
    total = jnp.zeros_like(parts[0][1])
    for j, (_, l) in enumerate(parts[:-1]):
        total = jnp.where(j < place, total + l, total)
    return total


def enter_body(place_ref, mine_ref, line_ref, wide_ref, send_ref):
    size = send_ref.shape[1]
    line = parts_of(line_ref, size)
    state = before(parts_of(wide_ref, size), place_ref[0])
    entering = jnp.exp(log_before(line, place_ref[2])) * state + before(line, place_ref[2])
    for j, (s, l) in enumerate(parts_of(mine_ref, size)):
        send_ref[j] = entering.astype(BF16)
        entering = jnp.exp(l) * entering + s


def raw_body(query_ref, log_ref, local_ref, enter_ref, raw_ref, square_ref):
    heads = query_ref.shape[1] // HD
    sums = block_sums(log_ref)
    ahead = jnp.zeros((1, heads), F32)
    for b, cum in enumerate(sums):
        rows = slice(b * BLK, (b + 1) * BLK)
        for h in range(heads):
            lanes = slice(h * HD, (h + 1) * HD)
            inter = dot(query_ref[rows, lanes], enter_ref[h], ((1,), (0,)))
            weight = jnp.exp(cum[:, h : h + 1] + ahead[:, h : h + 1])
            raw_ref[rows, lanes] = local_ref[rows, lanes] + weight * inter
        ahead = ahead + cum[BLK - 1 : BLK, :]
    raw = raw_ref[...]
    ones = jnp.ones((square_ref.shape[0], raw.shape[1]), F32)
    square_ref[...] = dot(ones, raw * raw, ((1,), (1,)), lax.Precision.HIGHEST)


def norm_body(columns, raw_ref, square_ref, gate_ref, gain_ref, out_ref):
    ones = jnp.full((square_ref.shape[0], HD), 1.0 / SAME, F32)
    total = dot(square_ref[...], ones, ((0,), (0,)), lax.Precision.HIGHEST)
    scale = lax.rsqrt(total / columns + EPS)
    for h in range(raw_ref.shape[1] // HD):
        lanes = slice(h * HD, (h + 1) * HD)
        gate = jax.nn.sigmoid(gate_ref[:, lanes].astype(F32))
        out_ref[:, lanes] = (raw_ref[:, lanes] * scale * gain_ref[:, lanes] * gate).astype(BF16)


def states(lin_key, lin_value, log_decay, soft_key, soft_value):
    tokens, features = lin_key.shape
    heads = features // HD
    logs = log_decay.T
    send, first, moving = call(
        states_body,
        (
            jax.ShapeDtypeStruct((QUAD, heads * HD // QUAD + LOG_ROWS, HD), BF16),
            jax.ShapeDtypeStruct((heads, HD, HD), F32),
            jax.ShapeDtypeStruct((tokens, 2 * soft_key.shape[1]), BF16),
        ),
        (lin_key, lin_value, logs, soft_key, soft_value),
        flops=4 * tokens * features * HD,
        moved=4 * tokens * features,
    )
    return logs, send, first, moving


def swap(array, groups):
    return lax.all_to_all(array, "seq", 0, 0, axis_index_groups=groups, tiled=True)


def gate_body(*refs):
    pass


def gate(array, *after):
    anywhere = pl.BlockSpec(memory_space=pl.ANY)
    return pl.pallas_call(
        gate_body,
        out_shape=jax.ShapeDtypeStruct(array.shape, array.dtype),
        in_specs=[anywhere] * (1 + len(after)),
        out_specs=anywhere,
        input_output_aliases={0: 0},
        compiler_params=pltpu.CompilerParams(vmem_limit_bytes=1024 * 1024),
        cost_estimate=pl.CostEstimate(flops=0, bytes_accessed=0, transcendentals=0),
    )(array, *after)


SCALE = math.log2(math.e) * HD ** (-0.5)


def attend_body(backs, opening, final, *refs):
    place_ref, docs_ref, query_ref = refs[:3]
    pieces = refs[3 : 3 + len(backs)]
    rest = refs[3 + len(backs) :]
    tokens, features = query_ref.shape
    heads = features // HD
    blocks = tokens // MBLK
    rows = heads * MBLK
    shard = place_ref[1]
    if opening:
        acc_ref, top_ref, sum_ref = rest
    elif final:
        acc_in, top_in, sum_in, out_ref, acc_ref, top_ref, sum_ref = rest
        acc_ref[...] = acc_in[...]
        top_ref[...] = top_in[...]
        sum_ref[...] = sum_in[...]
    else:
        acc_ref, top_ref, sum_ref = rest[3:]

    for i in range(blocks):
        mine = docs_ref[shard * blocks + i]

        def queries():
            return jnp.concatenate(
                [query_ref[i * MBLK : (i + 1) * MBLK, h * HD : (h + 1) * HD] for h in range(heads)],
                axis=0,
            )

        for back, piece in zip(backs, pieces):
            start = jnp.int32(0)
            for b in range(i if back == 0 else blocks):
                where = (shard - back) * blocks + b
                other = docs_ref[jnp.maximum(where, 0)]
                start = start + jnp.where((where >= 0) & (other == mine), 0, MBLK)
            if back == 0:
                width = (i + 1) * MBLK
                scores = dot(piece[:width, :HD], queries(), ((1,), (1,)))
                key = lax.broadcasted_iota(jnp.int32, (width, rows), 0)
                token = lax.broadcasted_iota(jnp.int32, (width, rows), 1)
                token = (token & (MBLK - 1)) + i * MBLK
                scores = jnp.where((key <= token) & (key >= start), scores, NEG)
                top = jnp.max(scores, axis=0, keepdims=True)
                probs = jnp.exp2(scores * SCALE - top * SCALE)
                sum_ref[i] = jnp.sum(probs, axis=0, keepdims=True)
                acc_ref[i] = dot(piece[:width, HD:], probs.astype(BF16), ((0,), (0,)))
                top_ref[i] = top
                continue

            def add(masked):
                scores = dot(piece[:, :HD], queries(), ((1,), (1,)))
                if masked:
                    key = lax.broadcasted_iota(jnp.int32, (tokens, rows), 0)
                    scores = jnp.where(key >= start, scores, NEG)
                old = top_ref[i]
                top = jnp.maximum(old, jnp.max(scores, axis=0, keepdims=True))
                probs = jnp.exp2(scores * SCALE - top * SCALE)
                shrink = jnp.exp2((old - top) * SCALE)
                sum_ref[i] = sum_ref[i] * shrink + jnp.sum(probs, axis=0, keepdims=True)
                added = dot(piece[:, HD:], probs.astype(BF16), ((0,), (0,)))
                acc_ref[i] = acc_ref[i] * shrink + added
                top_ref[i] = top

            pl.when(start == 0)(functools.partial(add, False))
            pl.when((start > 0) & (start < tokens))(functools.partial(add, True))

        if final:
            done = (acc_ref[i] / sum_ref[i]).T
            for h in range(heads):
                out_ref[i * MBLK : (i + 1) * MBLK, h * HD : (h + 1) * HD] = done[
                    h * MBLK : (h + 1) * MBLK
                ].astype(BF16)


def forward(array, steps):
    shards = lax.axis_size("seq")
    return lax.ppermute(array, "seq", [(s, s + steps) for s in range(shards - steps)])


def absorber(soft_query, doc_ids, place):
    tokens, features = soft_query.shape
    blocks = tokens // MBLK
    heads = features // HD
    rows = heads * MBLK
    carry = (
        jax.ShapeDtypeStruct((blocks, HD, rows), F32),
        jax.ShapeDtypeStruct((blocks, 1, rows), F32),
        jax.ShapeDtypeStruct((blocks, 1, rows), F32),
    )

    def absorb(state, backs, arrays, final=False):
        operands = (place, doc_ids, soft_query, *arrays, *state)
        aliases = {len(operands) - 3 + j: j for j in range(3)}
        return call(
            functools.partial(attend_body, backs, not state, final),
            jax.ShapeDtypeStruct((tokens, features), BF16) if final else carry,
            operands,
            smem=(0, 1),
            aliases=aliases if state and not final else None,
            scratch=tuple(pltpu.VMEM(c.shape, c.dtype) for c in carry) if final else (),
            flops=len(backs) * COST,
            moved=12 * tokens * features,
            exps=len(backs) * heads * tokens * tokens,
        )

    return absorb


def on_device(
    lin_query,
    lin_key,
    lin_value,
    lin_gate,
    log_decay,
    norm_gain,
    soft_query,
    soft_key,
    soft_value,
    doc_ids,
):
    tokens, features = lin_query.shape
    heads = features // HD
    shards = lax.axis_size("seq")
    peers = lax.axis_size("head")
    shard = lax.axis_index("seq")
    span = QUAD * QUAD
    place = jnp.stack([shard // span, shard, (shard % span) // QUAD]).astype(jnp.int32)
    near = [[QUAD * g + j for j in range(QUAD)] for g in range(shards // QUAD)]
    line = [
        [span * x + QUAD * a + b for a in range(QUAD)]
        for x in range(shards // span)
        for b in range(QUAD)
    ]
    wide = [[span * x + r for x in range(shards // span)] for r in range(span)]
    size = heads * HD // QUAD
    small = dict(flops=10 * heads * HD * HD, moved=4 * heads * HD * HD)
    hops = (DOC_MOST + tokens // MBLK - 2) // (tokens // MBLK)
    absorb = absorber(soft_query, doc_ids, place)

    logs, send, first, own = states(lin_key, lin_value, log_decay, soft_key, soft_value)
    mine = swap(send, near)
    back = [own]

    def hop(*after):
        if after:
            back[-1] = gate(back[-1], *after)
        back.append(forward(back[-1], 1))

    hop()
    local = call(
        local_body,
        jax.ShapeDtypeStruct((tokens, features), F32),
        (lin_query, lin_key, lin_value, logs, first),
        flops=4 * tokens * features * BLK,
        moved=10 * tokens * features,
    )
    state = absorb((), (0,), back[:1])
    hop(local, state[1])
    group = call(
        group_body,
        jax.ShapeDtypeStruct((QUAD, size + LOG_ROWS, HD), BF16),
        (mine,),
        **small,
    )
    lines = swap(group, line)
    hop(group)
    state = absorb(state, (1, 2), back[1:3])
    hop(state[1])
    total = call(
        group_body,
        jax.ShapeDtypeStruct((shards // span, size + 8, HD), F32),
        (lines,),
        **small,
    )
    wides = swap(total, wide)
    hop(total)
    state = absorb(state, (3, 4), back[3:5])
    hop(state[1])
    entering = call(
        enter_body,
        jax.ShapeDtypeStruct((QUAD, size, HD), BF16),
        (place, mine, lines, wides),
        smem=(0,),
        **small,
    )
    hop(entering)
    entering = swap(entering, near).reshape(heads, HD, HD)
    state = absorb(state, (5, 6), back[5:7])
    raw, squares = call(
        raw_body,
        (
            jax.ShapeDtypeStruct((tokens, features), F32),
            jax.ShapeDtypeStruct((peers * SAME, tokens), F32),
        ),
        (lin_query, logs, local, entering),
        flops=2 * tokens * features * HD,
        moved=10 * tokens * features,
    )
    squares = lax.all_to_all(squares, "head", 0, 0, tiled=True)
    lin_out = call(
        functools.partial(norm_body, float(features * peers)),
        jax.ShapeDtypeStruct((tokens, features), BF16),
        (raw, squares, lin_gate, norm_gain.reshape(1, features)),
        flops=8 * tokens * features,
        moved=8 * tokens * features,
        exps=tokens * features,
    )
    assert len(back) == hops + 1
    soft_out = absorb(state, tuple(range(7, hops + 1)), back[7:], True)
    return (lin_out, soft_out)


def solution(mesh):
    spread = P("seq", "head")
    return jax.shard_map(
        on_device,
        mesh=mesh,
        in_specs=(spread,) * 5 + (P("head"),) + (spread,) * 3 + (P(),),
        out_specs=(spread, spread),
        check_vma=False,
    )
```

```python
import functools
import math

import jax
import jax.numpy as jnp
import numpy as np
from jax import lax
from jax.experimental import pallas as pl
from jax.experimental.pallas import tpu as pltpu
from jax.sharding import PartitionSpec as P

HD = 128
BLK = 256
MBLK = 128
DOC_MOST = 29
EPS = 1e-06
NEG = -1e30
LOG_FLOOR = -1000.0
LOG_ROWS = 16
SAME = 8
QUAD = 4
F32 = jnp.float32
BF16 = jnp.bfloat16
VMEM_LIMIT = 8 * 1024 * 1024
ATTEND_LIMIT = 12 * 1024 * 1024
COST = 4 * 10**9


def call(
    body, outs, operands, *, flops, moved, exps=0, scratch=(), smem=(), aliases=None, after=()
):
    count = len(operands)
    if after:
        inner = body
        body = lambda *refs: inner(*refs[:count], *refs[count + len(after) :])
    operands = (*operands, *after)
    spaces = [pltpu.SMEM if i in smem else pltpu.VMEM for i in range(len(operands) - len(after))]
    specs = [pl.BlockSpec(memory_space=m) for m in spaces + [pl.ANY] * len(after)]
    return pl.pallas_call(
        body,
        out_shape=outs,
        in_specs=specs,
        out_specs=jax.tree.map(lambda _: pl.BlockSpec(memory_space=pltpu.VMEM), outs),
        scratch_shapes=list(scratch),
        input_output_aliases=aliases or {},
        compiler_params=pltpu.CompilerParams(vmem_limit_bytes=VMEM_LIMIT),
        cost_estimate=pl.CostEstimate(
            flops=int(flops), bytes_accessed=int(moved), transcendentals=int(exps)
        ),
    )(*operands)


def dot(a, b, dims, precision=None):
    return lax.dot_general(
        a, b, (dims, ((), ())), preferred_element_type=F32, precision=precision
    )


def split(x):
    high = x.astype(BF16)
    return high, (x - high.astype(F32)).astype(BF16)


def block_sums(log_ref):
    return [dot(tri, logs, ((1,), (1,)), lax.Precision.HIGHEST) for tri, logs in blocks_of(log_ref)]


def block_sums_across(log_ref):
    return [dot(logs, tri, ((1,), (1,)), lax.Precision.HIGHEST) for tri, logs in blocks_of(log_ref)]


def blocks_of(log_ref):
    rows = lax.broadcasted_iota(jnp.int32, (BLK, BLK), 0)
    cols = lax.broadcasted_iota(jnp.int32, (BLK, BLK), 1)
    tri = (rows >= cols).astype(F32)
    return [
        (tri, log_ref[:, b * BLK : (b + 1) * BLK]) for b in range(log_ref.shape[1] // BLK)
    ]


def log_rows(total):
    first = total.astype(BF16).astype(F32)
    second = (total - first).astype(BF16).astype(F32)
    third = total - first - second
    row = lax.broadcasted_iota(jnp.int32, (LOG_ROWS, HD), 0)
    packed = jnp.where(row == 0, first, jnp.where(row == 1, second, jnp.where(row == 2, third, 0.0)))
    return packed.astype(BF16)


def states_body(key_ref, value_ref, log_ref, soft_key_ref, soft_value_ref, send_ref, first_ref, moving_ref):
    moving_ref[:, : soft_key_ref.shape[1]] = soft_key_ref[...]
    moving_ref[:, soft_key_ref.shape[1] :] = soft_value_ref[...]
    heads = key_ref.shape[1] // HD
    sums = block_sums(log_ref)
    ends = [s[BLK - 1 : BLK, :] for s in sums]
    for h in range(heads):
        lanes = slice(h * HD, (h + 1) * HD)
        state = None
        total = jnp.zeros((1, 1), F32)
        for b, cum in enumerate(sums):
            rows = slice(b * BLK, (b + 1) * BLK)
            end = ends[b][:, h : h + 1]
            weight = jnp.exp(end - cum[:, h : h + 1])
            high, low = split(key_ref[rows, lanes].astype(F32) * weight)
            value = value_ref[rows, lanes]
            local = dot(high, value, ((0,), (0,))) + dot(low, value, ((0,), (0,)))
            if b == 0:
                first_ref[h] = local
                state = local
            else:
                state = jnp.exp(end) * state + local
            total = total + end
        total = jnp.broadcast_to(jnp.maximum(total, LOG_FLOOR), (1, HD))
        share, size = send_ref.shape[0] // heads, send_ref.shape[1] - LOG_ROWS
        for j in range(share):
            send_ref[h * share + j, :size, :] = state[j * size : (j + 1) * size].astype(BF16)
            send_ref[h * share + j, size:, :] = log_rows(total)


def local_body(query_ref, key_ref, value_ref, log_ref, first_ref, raw_ref):
    heads = key_ref.shape[1] // HD
    sums = block_sums(log_ref)
    across = block_sums_across(log_ref)
    rows_i = lax.broadcasted_iota(jnp.int32, (BLK, BLK), 0)
    cols_i = lax.broadcasted_iota(jnp.int32, (BLK, BLK), 1)
    causal = rows_i >= cols_i
    for b, cum in enumerate(sums):
        rows = slice(b * BLK, (b + 1) * BLK)
        for h in range(heads):
            lanes = slice(h * HD, (h + 1) * HD)
            column = cum[:, h : h + 1]
            query = query_ref[rows, lanes]
            gap = column - across[b][h : h + 1, :]
            weight = jnp.exp(jnp.where(causal, gap, NEG))
            scores = dot(query, key_ref[rows, lanes], ((1,), (1,)))
            mixed = (scores * weight).astype(BF16)
            raw = dot(mixed, value_ref[rows, lanes], ((1,), (0,)))
            if b > 0:
                high, low = split(first_ref[h])
                inter = dot(query, high, ((1,), (0,))) + dot(query, low, ((1,), (0,)))
                raw = raw + jnp.exp(column) * inter
            raw_ref[rows, lanes] = raw


def fold(parts):
    state, total = parts[0]
    for s, l in parts[1:]:
        state = jnp.exp(l) * state + s
        total = total + l
    return state, jnp.maximum(total, LOG_FLOOR)


def parts_of(got_ref, size):
    return [
        (
            got_ref[j, :size, :].astype(F32),
            jnp.sum(got_ref[j, size:, :].astype(F32), axis=0, keepdims=True),
        )
        for j in range(got_ref.shape[0])
    ]


def group_body(got_ref, send_ref):
    size = got_ref.shape[1] - LOG_ROWS
    state, total = fold(parts_of(got_ref, size))
    state = state.astype(send_ref.dtype)
    if send_ref.dtype == F32:
        row = lax.broadcasted_iota(jnp.int32, (send_ref.shape[1] - size, HD), 0)
        rows = jnp.where(row == 0, total, 0.0)
    else:
        rows = log_rows(total)
    for j in range(send_ref.shape[0]):
        send_ref[j, :size, :] = state
        send_ref[j, size:, :] = rows


def before(parts, place):
    state = jnp.zeros_like(parts[0][0])
    for j, (s, l) in enumerate(parts[:-1]):
        state = jnp.where(j < place, jnp.exp(l) * state + s, state)
    return state


def log_before(parts, place):
    total = jnp.zeros_like(parts[0][1])
    for j, (_, l) in enumerate(parts[:-1]):
        total = jnp.where(j < place, total + l, total)
    return total


def enter_body(place_ref, mine_ref, line_ref, wide_ref, send_ref):
    size = send_ref.shape[1]
    line = parts_of(line_ref, size)
    state = before(parts_of(wide_ref, size), place_ref[0])
    entering = jnp.exp(log_before(line, place_ref[2])) * state + before(line, place_ref[2])
    for j, (s, l) in enumerate(parts_of(mine_ref, size)):
        send_ref[j] = entering.astype(BF16)
        entering = jnp.exp(l) * entering + s


def raw_body(query_ref, log_ref, local_ref, enter_ref, raw_ref, square_ref):
    heads = query_ref.shape[1] // HD
    sums = block_sums(log_ref)
    ahead = jnp.zeros((1, heads), F32)
    for b, cum in enumerate(sums):
        rows = slice(b * BLK, (b + 1) * BLK)
        for h in range(heads):
            lanes = slice(h * HD, (h + 1) * HD)
            inter = dot(query_ref[rows, lanes], enter_ref[h], ((1,), (0,)))
            weight = jnp.exp(cum[:, h : h + 1] + ahead[:, h : h + 1])
            raw_ref[rows, lanes] = local_ref[rows, lanes] + weight * inter
        ahead = ahead + cum[BLK - 1 : BLK, :]
    raw = raw_ref[...]
    ones = jnp.ones((square_ref.shape[0], raw.shape[1]), F32)
    square_ref[...] = dot(ones, raw * raw, ((1,), (1,)), lax.Precision.HIGHEST)


def norm_body(columns, raw_ref, square_ref, gate_ref, gain_ref, out_ref):
    ones = jnp.full((square_ref.shape[0], HD), 1.0 / SAME, F32)
    total = dot(square_ref[...], ones, ((0,), (0,)), lax.Precision.HIGHEST)
    scale = lax.rsqrt(total / columns + EPS)
    for h in range(raw_ref.shape[1] // HD):
        lanes = slice(h * HD, (h + 1) * HD)
        gate = jax.nn.sigmoid(gate_ref[:, lanes].astype(F32))
        out_ref[:, lanes] = (raw_ref[:, lanes] * scale * gain_ref[:, lanes] * gate).astype(BF16)


def states(lin_key, lin_value, log_decay, soft_key, soft_value):
    tokens, features = lin_key.shape
    heads = features // HD
    logs = log_decay.T
    send, first, moving = call(
        states_body,
        (
            jax.ShapeDtypeStruct((QUAD, heads * HD // QUAD + LOG_ROWS, HD), BF16),
            jax.ShapeDtypeStruct((heads, HD, HD), F32),
            jax.ShapeDtypeStruct((tokens, 2 * soft_key.shape[1]), BF16),
        ),
        (lin_key, lin_value, logs, soft_key, soft_value),
        flops=4 * tokens * features * HD,
        moved=4 * tokens * features,
    )
    return logs, send, first, moving


def swap(array, groups):
    return lax.all_to_all(array, "seq", 0, 0, axis_index_groups=groups, tiled=True)


def gate_body(*refs):
    pass


def gate(array, *after):
    anywhere = pl.BlockSpec(memory_space=pl.ANY)
    return pl.pallas_call(
        gate_body,
        out_shape=jax.ShapeDtypeStruct(array.shape, array.dtype),
        in_specs=[anywhere] * (1 + len(after)),
        out_specs=anywhere,
        input_output_aliases={0: 0},
        compiler_params=pltpu.CompilerParams(vmem_limit_bytes=1024 * 1024),
        cost_estimate=pl.CostEstimate(flops=0, bytes_accessed=0, transcendentals=0),
    )(array, *after)


SCALE = math.log2(math.e) * HD ** (-0.5)


def attend_body(backs, opening, final, *refs):
    place_ref, docs_ref, query_hbm = refs[:3]
    pieces = refs[3 : 3 + len(backs)]
    rest = refs[3 + len(backs) :]
    acc_hbm = None if opening else rest[0]
    out_ref, query_ref, acc_ref, query_sem, in_sem, out_sem = rest[-6:]
    tokens, features = query_hbm.shape
    heads = features // HD
    blocks = tokens // MBLK
    rows = heads * MBLK
    shard = place_ref[1]

    begins = []
    for i in range(blocks):
        mine = docs_ref[shard * blocks + i]
        begins.append([])
        for back in backs:
            start = jnp.int32(0)
            for b in range(i if back == 0 else blocks):
                where = (shard - back) * blocks + b
                other = docs_ref[jnp.maximum(where, 0)]
                start = start + jnp.where((where >= 0) & (other == mine), 0, MBLK)
            begins[i].append(start)
    reached = [functools.reduce(jnp.minimum, starts) < tokens for starts in begins]

    def query_copy(i):
        return pltpu.make_async_copy(
            query_hbm.at[pl.ds(i * MBLK, MBLK), :], query_ref.at[i], query_sem.at[i]
        )

    def in_copy(i):
        return pltpu.make_async_copy(acc_hbm.at[i], acc_ref.at[i], in_sem.at[i])

    def out_copy(i):
        return pltpu.make_async_copy(acc_ref.at[i], out_ref.at[i], out_sem.at[i])

    for i in range(blocks):
        if final:
            in_copy(i).start()

        @pl.when(reached[i])
        def _():
            query_copy(i).start()
            if not opening and not final:
                in_copy(i).start()

    for i in range(blocks):
        if final:
            in_copy(i).wait()

        @pl.when(reached[i])
        def _():
            query_copy(i).wait()
            if not opening and not final:
                in_copy(i).wait()

        def queries():
            return jnp.concatenate(
                [query_ref[i, :, h * HD : (h + 1) * HD] for h in range(heads)], axis=0
            )

        for back, piece, start in zip(backs, pieces, begins[i]):
            if back == 0:
                width = (i + 1) * MBLK
                scores = dot(piece[:width, :HD], queries(), ((1,), (1,)))
                key = lax.broadcasted_iota(jnp.int32, (width, rows), 0)
                token = lax.broadcasted_iota(jnp.int32, (width, rows), 1)
                token = (token & (MBLK - 1)) + i * MBLK
                scores = jnp.where((key <= token) & (key >= start), scores, NEG)
                top = jnp.max(scores, axis=0, keepdims=True)
                probs = jnp.exp2(scores * SCALE - top * SCALE)
                total = jnp.sum(probs, axis=0, keepdims=True)
                acc_ref[i, :HD, :] = dot(piece[:width, HD:], probs.astype(BF16), ((0,), (0,)))
                acc_ref[i, HD : HD + 8, :] = jnp.broadcast_to(top, (8, rows))
                acc_ref[i, HD + 8 :, :] = jnp.broadcast_to(total, (8, rows))
                continue

            def add(masked):
                scores = dot(piece[:, :HD], queries(), ((1,), (1,)))
                if masked:
                    key = lax.broadcasted_iota(jnp.int32, (tokens, rows), 0)
                    scores = jnp.where(key >= start, scores, NEG)
                old = acc_ref[i, HD : HD + 1, :]
                top = jnp.maximum(old, jnp.max(scores, axis=0, keepdims=True))
                probs = jnp.exp2(scores * SCALE - top * SCALE)
                shrink = jnp.exp2((old - top) * SCALE)
                total = acc_ref[i, HD + 8 : HD + 9, :] * shrink + jnp.sum(
                    probs, axis=0, keepdims=True
                )
                added = dot(piece[:, HD:], probs.astype(BF16), ((0,), (0,)))
                acc_ref[i, :HD, :] = acc_ref[i, :HD, :] * shrink + added
                acc_ref[i, HD : HD + 8, :] = jnp.broadcast_to(top, (8, rows))
                acc_ref[i, HD + 8 :, :] = jnp.broadcast_to(total, (8, rows))

            pl.when(start == 0)(functools.partial(add, False))
            pl.when((start > 0) & (start < tokens))(functools.partial(add, True))

        if final:
            done = (acc_ref[i, :HD, :] / acc_ref[i, HD + 8 : HD + 9, :]).T
            for h in range(heads):
                out_ref[i * MBLK : (i + 1) * MBLK, h * HD : (h + 1) * HD] = done[
                    h * MBLK : (h + 1) * MBLK
                ].astype(BF16)
        else:

            @pl.when(reached[i])
            def _():
                out_copy(i).start()

    if not final:
        for i in range(blocks):

            @pl.when(reached[i])
            def _():
                out_copy(i).wait()


def forward(array, steps):
    shards = lax.axis_size("seq")
    return lax.ppermute(array, "seq", [(s, s + steps) for s in range(shards - steps)])


def absorber(soft_query, doc_ids, place):
    tokens, features = soft_query.shape
    blocks = tokens // MBLK
    heads = features // HD
    rows = heads * MBLK
    carry = jax.ShapeDtypeStruct((blocks, HD + 16, rows), F32)
    anywhere = pl.BlockSpec(memory_space=pl.ANY)
    scalars = pl.BlockSpec(memory_space=pltpu.SMEM)
    vectors = pl.BlockSpec(memory_space=pltpu.VMEM)

    def absorb(state, backs, arrays, final=False):
        opening = state is None
        held = [] if opening else [state]
        return pl.pallas_call(
            functools.partial(attend_body, backs, opening, final),
            out_shape=jax.ShapeDtypeStruct((tokens, features), BF16) if final else carry,
            in_specs=[scalars] * 2
            + [anywhere]
            + [vectors] * len(backs)
            + [anywhere] * len(held),
            out_specs=vectors if final else anywhere,
            scratch_shapes=[
                pltpu.VMEM((blocks, MBLK, features), BF16),
                pltpu.VMEM(carry.shape, F32),
                pltpu.SemaphoreType.DMA((blocks,)),
                pltpu.SemaphoreType.DMA((blocks,)),
                pltpu.SemaphoreType.DMA((blocks,)),
            ],
            input_output_aliases={3 + len(backs): 0} if held and not final else {},
            compiler_params=pltpu.CompilerParams(vmem_limit_bytes=ATTEND_LIMIT),
            cost_estimate=pl.CostEstimate(
                flops=len(backs) * COST,
                bytes_accessed=12 * tokens * features,
                transcendentals=len(backs) * heads * tokens * tokens,
            ),
        )(place, doc_ids, soft_query, *arrays, *held)

    return absorb


def on_device(
    lin_query,
    lin_key,
    lin_value,
    lin_gate,
    log_decay,
    norm_gain,
    soft_query,
    soft_key,
    soft_value,
    doc_ids,
):
    tokens, features = lin_query.shape
    heads = features // HD
    shards = lax.axis_size("seq")
    peers = lax.axis_size("head")
    shard = lax.axis_index("seq")
    span = QUAD * QUAD
    place = jnp.stack([shard // span, shard, (shard % span) // QUAD]).astype(jnp.int32)
    near = [[QUAD * g + j for j in range(QUAD)] for g in range(shards // QUAD)]
    line = [
        [span * x + QUAD * a + b for a in range(QUAD)]
        for x in range(shards // span)
        for b in range(QUAD)
    ]
    wide = [[span * x + r for x in range(shards // span)] for r in range(span)]
    size = heads * HD // QUAD
    small = dict(flops=10 * heads * HD * HD, moved=4 * heads * HD * HD)
    hops = (DOC_MOST + tokens // MBLK - 2) // (tokens // MBLK)
    absorb = absorber(soft_query, doc_ids, place)

    logs, send, first, own = states(lin_key, lin_value, log_decay, soft_key, soft_value)
    mine = swap(send, near)
    back = [own]

    def hop(*after):
        if after:
            back[-1] = gate(back[-1], *after)
        back.append(forward(back[-1], 1))

    hop()
    local = call(
        local_body,
        jax.ShapeDtypeStruct((tokens, features), F32),
        (lin_query, lin_key, lin_value, logs, first),
        flops=4 * tokens * features * BLK,
        moved=10 * tokens * features,
    )
    state = absorb(None, (0,), back[:1])
    hop(local, state)
    group = call(
        group_body,
        jax.ShapeDtypeStruct((QUAD, size + LOG_ROWS, HD), BF16),
        (mine,),
        **small,
    )
    lines = swap(group, line)
    hop(group)
    state = absorb(state, (1, 2), back[1:3])
    hop(state)
    total = call(
        group_body,
        jax.ShapeDtypeStruct((shards // span, size + 8, HD), F32),
        (lines,),
        **small,
    )
    wides = swap(total, wide)
    hop(total)
    state = absorb(state, (3, 4), back[3:5])
    hop(state)
    entering = call(
        enter_body,
        jax.ShapeDtypeStruct((QUAD, size, HD), BF16),
        (place, mine, lines, wides),
        smem=(0,),
        **small,
    )
    hop(entering)
    entering = swap(entering, near).reshape(heads, HD, HD)
    state = absorb(state, (5, 6), back[5:7])
    raw, squares = call(
        raw_body,
        (
            jax.ShapeDtypeStruct((tokens, features), F32),
            jax.ShapeDtypeStruct((peers * SAME, tokens), F32),
        ),
        (lin_query, logs, local, entering),
        flops=2 * tokens * features * HD,
        moved=10 * tokens * features,
    )
    squares = lax.all_to_all(squares, "head", 0, 0, tiled=True)
    lin_out = call(
        functools.partial(norm_body, float(features * peers)),
        jax.ShapeDtypeStruct((tokens, features), BF16),
        (raw, squares, lin_gate, norm_gain.reshape(1, features)),
        flops=8 * tokens * features,
        moved=8 * tokens * features,
        exps=tokens * features,
    )
    assert len(back) == hops + 1
    soft_out = absorb(state, tuple(range(7, hops + 1)), back[7:], True)
    return (lin_out, soft_out)


def solution(mesh):
    spread = P("seq", "head")
    return jax.shard_map(
        on_device,
        mesh=mesh,
        in_specs=(spread,) * 5 + (P("head"),) + (spread,) * 3 + (P(),),
        out_specs=(spread, spread),
        check_vma=False,
    )
```

```python
import functools
import math

import jax
import jax.numpy as jnp
import numpy as np
from jax import lax
from jax.experimental import pallas as pl
from jax.experimental.pallas import tpu as pltpu
from jax.sharding import PartitionSpec as P

HD = 128
BLK = 256
MBLK = 128
DOC_MOST = 29
EPS = 1e-06
NEG = -1e30
LOG_FLOOR = -1000.0
LOG_ROWS = 16
SAME = 8
QUAD = 4
F32 = jnp.float32
BF16 = jnp.bfloat16
VMEM_LIMIT = 8 * 1024 * 1024
ATTEND_LIMIT = 12 * 1024 * 1024
WHOLE_LIMIT = (64 * 1024 - 512) * 1024
COST = 4 * 10**9


def call(
    body, outs, operands, *, flops, moved, exps=0, scratch=(), smem=(), aliases=None, after=()
):
    count = len(operands)
    if after:
        inner = body
        body = lambda *refs: inner(*refs[:count], *refs[count + len(after) :])
    operands = (*operands, *after)
    spaces = [pltpu.SMEM if i in smem else pltpu.VMEM for i in range(len(operands) - len(after))]
    specs = [pl.BlockSpec(memory_space=m) for m in spaces + [pl.ANY] * len(after)]
    return pl.pallas_call(
        body,
        out_shape=outs,
        in_specs=specs,
        out_specs=jax.tree.map(lambda _: pl.BlockSpec(memory_space=pltpu.VMEM), outs),
        scratch_shapes=list(scratch),
        input_output_aliases=aliases or {},
        compiler_params=pltpu.CompilerParams(vmem_limit_bytes=VMEM_LIMIT),
        cost_estimate=pl.CostEstimate(
            flops=int(flops), bytes_accessed=int(moved), transcendentals=int(exps)
        ),
    )(*operands)


def dot(a, b, dims, precision=None):
    return lax.dot_general(
        a, b, (dims, ((), ())), preferred_element_type=F32, precision=precision
    )


def split(x):
    high = x.astype(BF16)
    return high, (x - high.astype(F32)).astype(BF16)


def block_sums(log_ref):
    return [dot(tri, logs, ((1,), (1,)), lax.Precision.HIGHEST) for tri, logs in blocks_of(log_ref)]


def block_sums_across(log_ref):
    return [dot(logs, tri, ((1,), (1,)), lax.Precision.HIGHEST) for tri, logs in blocks_of(log_ref)]


def blocks_of(log_ref):
    rows = lax.broadcasted_iota(jnp.int32, (BLK, BLK), 0)
    cols = lax.broadcasted_iota(jnp.int32, (BLK, BLK), 1)
    tri = (rows >= cols).astype(F32)
    return [
        (tri, log_ref[:, b * BLK : (b + 1) * BLK]) for b in range(log_ref.shape[1] // BLK)
    ]


def log_rows(total):
    first = total.astype(BF16).astype(F32)
    second = (total - first).astype(BF16).astype(F32)
    third = total - first - second
    row = lax.broadcasted_iota(jnp.int32, (LOG_ROWS, HD), 0)
    packed = jnp.where(row == 0, first, jnp.where(row == 1, second, jnp.where(row == 2, third, 0.0)))
    return packed.astype(BF16)


def join_body(key_hbm, value_hbm, moving_ref, sems):
    width = key_hbm.shape[1]
    copies = [
        pltpu.make_async_copy(key_hbm, moving_ref.at[:, pl.ds(0, width)], sems.at[0]),
        pltpu.make_async_copy(value_hbm, moving_ref.at[:, pl.ds(width, width)], sems.at[1]),
    ]
    for copy in copies:
        copy.start()
    for copy in copies:
        copy.wait()


def states_body(key_hbm, value_hbm, log_hbm, *rest):
    send_ref, first_ref, key_ref, value_ref, log_ref, sems = rest[-6:]
    copies = [
        pltpu.make_async_copy(log_hbm, log_ref, sems.at[0]),
        pltpu.make_async_copy(key_hbm, key_ref, sems.at[1]),
        pltpu.make_async_copy(value_hbm, value_ref, sems.at[2]),
    ]
    for copy in copies:
        copy.start()
    for copy in copies:
        copy.wait()
    heads = key_ref.shape[1] // HD
    sums = block_sums(log_ref)
    ends = [s[BLK - 1 : BLK, :] for s in sums]
    for h in range(heads):
        lanes = slice(h * HD, (h + 1) * HD)
        state = None
        total = jnp.zeros((1, 1), F32)
        for b, cum in enumerate(sums):
            rows = slice(b * BLK, (b + 1) * BLK)
            end = ends[b][:, h : h + 1]
            weight = jnp.exp(end - cum[:, h : h + 1])
            high, low = split(key_ref[rows, lanes].astype(F32) * weight)
            value = value_ref[rows, lanes]
            local = dot(high, value, ((0,), (0,))) + dot(low, value, ((0,), (0,)))
            if b == 0:
                first_ref[h] = local
                state = local
            else:
                state = jnp.exp(end) * state + local
            total = total + end
        total = jnp.broadcast_to(jnp.maximum(total, LOG_FLOOR), (1, HD))
        share, size = send_ref.shape[0] // heads, send_ref.shape[1] - LOG_ROWS
        for j in range(share):
            send_ref[h * share + j, :size, :] = state[j * size : (j + 1) * size].astype(BF16)
            send_ref[h * share + j, size:, :] = log_rows(total)


def local_body(query_ref, key_ref, value_ref, log_ref, first_ref, raw_ref):
    heads = key_ref.shape[1] // HD
    sums = block_sums(log_ref)
    across = block_sums_across(log_ref)
    rows_i = lax.broadcasted_iota(jnp.int32, (BLK, BLK), 0)
    cols_i = lax.broadcasted_iota(jnp.int32, (BLK, BLK), 1)
    causal = rows_i >= cols_i
    for b, cum in enumerate(sums):
        rows = slice(b * BLK, (b + 1) * BLK)
        for h in range(heads):
            lanes = slice(h * HD, (h + 1) * HD)
            column = cum[:, h : h + 1]
            query = query_ref[rows, lanes]
            gap = column - across[b][h : h + 1, :]
            weight = jnp.exp(jnp.where(causal, gap, NEG))
            scores = dot(query, key_ref[rows, lanes], ((1,), (1,)))
            mixed = (scores * weight).astype(BF16)
            raw = dot(mixed, value_ref[rows, lanes], ((1,), (0,)))
            if b > 0:
                high, low = split(first_ref[h])
                inter = dot(query, high, ((1,), (0,))) + dot(query, low, ((1,), (0,)))
                raw = raw + jnp.exp(column) * inter
            raw_ref[rows, lanes] = raw


def fold(parts):
    state, total = parts[0]
    for s, l in parts[1:]:
        state = jnp.exp(l) * state + s
        total = total + l
    return state, jnp.maximum(total, LOG_FLOOR)


def parts_of(got_ref, size):
    return [
        (
            got_ref[j, :size, :].astype(F32),
            jnp.sum(got_ref[j, size:, :].astype(F32), axis=0, keepdims=True),
        )
        for j in range(got_ref.shape[0])
    ]


def group_body(got_ref, send_ref):
    size = got_ref.shape[1] - LOG_ROWS
    state, total = fold(parts_of(got_ref, size))
    state = state.astype(send_ref.dtype)
    if send_ref.dtype == F32:
        row = lax.broadcasted_iota(jnp.int32, (send_ref.shape[1] - size, HD), 0)
        rows = jnp.where(row == 0, total, 0.0)
    else:
        rows = log_rows(total)
    for j in range(send_ref.shape[0]):
        send_ref[j, :size, :] = state
        send_ref[j, size:, :] = rows


def before(parts, place):
    state = jnp.zeros_like(parts[0][0])
    for j, (s, l) in enumerate(parts[:-1]):
        state = jnp.where(j < place, jnp.exp(l) * state + s, state)
    return state


def log_before(parts, place):
    total = jnp.zeros_like(parts[0][1])
    for j, (_, l) in enumerate(parts[:-1]):
        total = jnp.where(j < place, total + l, total)
    return total


def enter_body(place_ref, mine_ref, line_ref, wide_ref, send_ref):
    size = send_ref.shape[1]
    line = parts_of(line_ref, size)
    state = before(parts_of(wide_ref, size), place_ref[0])
    entering = jnp.exp(log_before(line, place_ref[2])) * state + before(line, place_ref[2])
    for j, (s, l) in enumerate(parts_of(mine_ref, size)):
        send_ref[j] = entering.astype(BF16)
        entering = jnp.exp(l) * entering + s


def raw_body(query_ref, log_ref, local_ref, enter_ref, raw_ref, square_ref):
    heads = query_ref.shape[1] // HD
    sums = block_sums(log_ref)
    ahead = jnp.zeros((1, heads), F32)
    for b, cum in enumerate(sums):
        rows = slice(b * BLK, (b + 1) * BLK)
        for h in range(heads):
            lanes = slice(h * HD, (h + 1) * HD)
            inter = dot(query_ref[rows, lanes], enter_ref[h], ((1,), (0,)))
            weight = jnp.exp(cum[:, h : h + 1] + ahead[:, h : h + 1])
            raw_ref[rows, lanes] = local_ref[rows, lanes] + weight * inter
        ahead = ahead + cum[BLK - 1 : BLK, :]
    raw = raw_ref[...]
    ones = jnp.ones((square_ref.shape[0], raw.shape[1]), F32)
    square_ref[...] = dot(ones, raw * raw, ((1,), (1,)), lax.Precision.HIGHEST)


def norm_body(columns, raw_ref, square_ref, gate_ref, gain_ref, out_ref):
    ones = jnp.full((square_ref.shape[0], HD), 1.0 / SAME, F32)
    total = dot(square_ref[...], ones, ((0,), (0,)), lax.Precision.HIGHEST)
    scale = lax.rsqrt(total / columns + EPS)
    for h in range(raw_ref.shape[1] // HD):
        lanes = slice(h * HD, (h + 1) * HD)
        gate = jax.nn.sigmoid(gate_ref[:, lanes].astype(F32))
        out_ref[:, lanes] = (raw_ref[:, lanes] * scale * gain_ref[:, lanes] * gate).astype(BF16)


def states(lin_key, lin_value, log_decay, soft_key, soft_value):
    tokens, features = lin_key.shape
    heads = features // HD
    logs = log_decay.T
    anywhere = pl.BlockSpec(memory_space=pl.ANY)
    vectors = pl.BlockSpec(memory_space=pltpu.VMEM)
    limit = pltpu.CompilerParams(vmem_limit_bytes=WHOLE_LIMIT)
    moving = pl.pallas_call(
        join_body,
        out_shape=jax.ShapeDtypeStruct((tokens, 2 * soft_key.shape[1]), BF16),
        in_specs=[anywhere] * 2,
        out_specs=vectors,
        scratch_shapes=[pltpu.SemaphoreType.DMA((2,))],
        compiler_params=limit,
        cost_estimate=pl.CostEstimate(
            flops=0, bytes_accessed=8 * soft_key.size, transcendentals=0
        ),
    )(soft_key, soft_value)
    send, first = pl.pallas_call(
        states_body,
        out_shape=(
            jax.ShapeDtypeStruct((QUAD, heads * HD // QUAD + LOG_ROWS, HD), BF16),
            jax.ShapeDtypeStruct((heads, HD, HD), F32),
        ),
        in_specs=[anywhere] * 4,
        out_specs=(vectors, vectors),
        scratch_shapes=[
            pltpu.VMEM((tokens, features), BF16),
            pltpu.VMEM((tokens, features), BF16),
            pltpu.VMEM(logs.shape, F32),
            pltpu.SemaphoreType.DMA((3,)),
        ],
        compiler_params=limit,
        cost_estimate=pl.CostEstimate(
            flops=4 * tokens * features * HD,
            bytes_accessed=4 * tokens * features,
            transcendentals=0,
        ),
    )(lin_key, lin_value, logs, moving)
    return logs, send, first, moving


def swap(array, groups):
    return lax.all_to_all(array, "seq", 0, 0, axis_index_groups=groups, tiled=True)


def gate_body(*refs):
    pass


def gate(array, *after):
    anywhere = pl.BlockSpec(memory_space=pl.ANY)
    return pl.pallas_call(
        gate_body,
        out_shape=jax.ShapeDtypeStruct(array.shape, array.dtype),
        in_specs=[anywhere] * (1 + len(after)),
        out_specs=anywhere,
        input_output_aliases={0: 0},
        compiler_params=pltpu.CompilerParams(vmem_limit_bytes=1024 * 1024),
        cost_estimate=pl.CostEstimate(flops=0, bytes_accessed=0, transcendentals=0),
    )(array, *after)


SCALE = math.log2(math.e) * HD ** (-0.5)


def attend_body(backs, opening, final, *refs):
    place_ref, docs_ref, query_hbm = refs[:3]
    pieces = refs[3 : 3 + len(backs)]
    rest = refs[3 + len(backs) :]
    acc_hbm = None if opening else rest[0]
    out_ref, query_ref, acc_ref, query_sem, in_sem, out_sem = rest[-6:]
    tokens, features = query_hbm.shape
    heads = features // HD
    blocks = tokens // MBLK
    rows = heads * MBLK
    shard = place_ref[1]

    begins = []
    for i in range(blocks):
        mine = docs_ref[shard * blocks + i]
        begins.append([])
        for back in backs:
            start = jnp.int32(0)
            for b in range(i if back == 0 else blocks):
                where = (shard - back) * blocks + b
                other = docs_ref[jnp.maximum(where, 0)]
                start = start + jnp.where((where >= 0) & (other == mine), 0, MBLK)
            begins[i].append(start)
    reached = [functools.reduce(jnp.minimum, starts) < tokens for starts in begins]

    def query_copy(i):
        return pltpu.make_async_copy(
            query_hbm.at[pl.ds(i * MBLK, MBLK), :], query_ref.at[i], query_sem.at[i]
        )

    def in_copy(i):
        return pltpu.make_async_copy(acc_hbm.at[i], acc_ref.at[i], in_sem.at[i])

    def out_copy(i):
        return pltpu.make_async_copy(acc_ref.at[i], out_ref.at[i], out_sem.at[i])

    for i in range(blocks):
        if final:
            in_copy(i).start()

        @pl.when(reached[i])
        def _():
            query_copy(i).start()
            if not opening and not final:
                in_copy(i).start()

    for i in range(blocks):
        if final:
            in_copy(i).wait()

        @pl.when(reached[i])
        def _():
            query_copy(i).wait()
            if not opening and not final:
                in_copy(i).wait()

        def queries():
            return jnp.concatenate(
                [query_ref[i, :, h * HD : (h + 1) * HD] for h in range(heads)], axis=0
            )

        for back, piece, start in zip(backs, pieces, begins[i]):
            if back == 0:
                width = (i + 1) * MBLK
                scores = dot(piece[:width, :HD], queries(), ((1,), (1,)))
                key = lax.broadcasted_iota(jnp.int32, (width, rows), 0)
                token = lax.broadcasted_iota(jnp.int32, (width, rows), 1)
                token = (token & (MBLK - 1)) + i * MBLK
                scores = jnp.where((key <= token) & (key >= start), scores, NEG)
                top = jnp.max(scores, axis=0, keepdims=True)
                probs = jnp.exp2(scores * SCALE - top * SCALE)
                total = jnp.sum(probs, axis=0, keepdims=True)
                acc_ref[i, :HD, :] = dot(piece[:width, HD:], probs.astype(BF16), ((0,), (0,)))
                acc_ref[i, HD : HD + 8, :] = jnp.broadcast_to(top, (8, rows))
                acc_ref[i, HD + 8 :, :] = jnp.broadcast_to(total, (8, rows))
                continue

            def add(masked):
                scores = dot(piece[:, :HD], queries(), ((1,), (1,)))
                if masked:
                    key = lax.broadcasted_iota(jnp.int32, (tokens, rows), 0)
                    scores = jnp.where(key >= start, scores, NEG)
                old = acc_ref[i, HD : HD + 1, :]
                top = jnp.maximum(old, jnp.max(scores, axis=0, keepdims=True))
                probs = jnp.exp2(scores * SCALE - top * SCALE)
                shrink = jnp.exp2((old - top) * SCALE)
                total = acc_ref[i, HD + 8 : HD + 9, :] * shrink + jnp.sum(
                    probs, axis=0, keepdims=True
                )
                added = dot(piece[:, HD:], probs.astype(BF16), ((0,), (0,)))
                acc_ref[i, :HD, :] = acc_ref[i, :HD, :] * shrink + added
                acc_ref[i, HD : HD + 8, :] = jnp.broadcast_to(top, (8, rows))
                acc_ref[i, HD + 8 :, :] = jnp.broadcast_to(total, (8, rows))

            pl.when(start == 0)(functools.partial(add, False))
            pl.when((start > 0) & (start < tokens))(functools.partial(add, True))

        if final:
            done = (acc_ref[i, :HD, :] / acc_ref[i, HD + 8 : HD + 9, :]).T
            for h in range(heads):
                out_ref[i * MBLK : (i + 1) * MBLK, h * HD : (h + 1) * HD] = done[
                    h * MBLK : (h + 1) * MBLK
                ].astype(BF16)
        else:

            @pl.when(reached[i])
            def _():
                out_copy(i).start()

    if not final:
        for i in range(blocks):

            @pl.when(reached[i])
            def _():
                out_copy(i).wait()


def forward(array, steps):
    shards = lax.axis_size("seq")
    return lax.ppermute(array, "seq", [(s, s + steps) for s in range(shards - steps)])


def absorber(soft_query, doc_ids, place):
    tokens, features = soft_query.shape
    blocks = tokens // MBLK
    heads = features // HD
    rows = heads * MBLK
    carry = jax.ShapeDtypeStruct((blocks, HD + 16, rows), F32)
    anywhere = pl.BlockSpec(memory_space=pl.ANY)
    scalars = pl.BlockSpec(memory_space=pltpu.SMEM)
    vectors = pl.BlockSpec(memory_space=pltpu.VMEM)

    def absorb(state, backs, arrays, final=False):
        opening = state is None
        held = [] if opening else [state]
        return pl.pallas_call(
            functools.partial(attend_body, backs, opening, final),
            out_shape=jax.ShapeDtypeStruct((tokens, features), BF16) if final else carry,
            in_specs=[scalars] * 2
            + [anywhere]
            + [vectors] * len(backs)
            + [anywhere] * len(held),
            out_specs=vectors if final else anywhere,
            scratch_shapes=[
                pltpu.VMEM((blocks, MBLK, features), BF16),
                pltpu.VMEM(carry.shape, F32),
                pltpu.SemaphoreType.DMA((blocks,)),
                pltpu.SemaphoreType.DMA((blocks,)),
                pltpu.SemaphoreType.DMA((blocks,)),
            ],
            input_output_aliases={3 + len(backs): 0} if held and not final else {},
            compiler_params=pltpu.CompilerParams(vmem_limit_bytes=ATTEND_LIMIT),
            cost_estimate=pl.CostEstimate(
                flops=len(backs) * COST,
                bytes_accessed=12 * tokens * features,
                transcendentals=len(backs) * heads * tokens * tokens,
            ),
        )(place, doc_ids, soft_query, *arrays, *held)

    return absorb


def on_device(
    lin_query,
    lin_key,
    lin_value,
    lin_gate,
    log_decay,
    norm_gain,
    soft_query,
    soft_key,
    soft_value,
    doc_ids,
):
    tokens, features = lin_query.shape
    heads = features // HD
    shards = lax.axis_size("seq")
    peers = lax.axis_size("head")
    shard = lax.axis_index("seq")
    span = QUAD * QUAD
    place = jnp.stack([shard // span, shard, (shard % span) // QUAD]).astype(jnp.int32)
    near = [[QUAD * g + j for j in range(QUAD)] for g in range(shards // QUAD)]
    line = [
        [span * x + QUAD * a + b for a in range(QUAD)]
        for x in range(shards // span)
        for b in range(QUAD)
    ]
    wide = [[span * x + r for x in range(shards // span)] for r in range(span)]
    size = heads * HD // QUAD
    small = dict(flops=10 * heads * HD * HD, moved=4 * heads * HD * HD)
    hops = (DOC_MOST + tokens // MBLK - 2) // (tokens // MBLK)
    absorb = absorber(soft_query, doc_ids, place)

    logs, send, first, own = states(lin_key, lin_value, log_decay, soft_key, soft_value)
    mine = swap(send, near)
    back = [own]

    def hop(*after):
        if after:
            back[-1] = gate(back[-1], *after)
        back.append(forward(back[-1], 1))

    hop()
    local = call(
        local_body,
        jax.ShapeDtypeStruct((tokens, features), F32),
        (lin_query, lin_key, lin_value, logs, first),
        flops=4 * tokens * features * BLK,
        moved=10 * tokens * features,
    )
    state = absorb(None, (0,), back[:1])
    hop(local, state)
    group = call(
        group_body,
        jax.ShapeDtypeStruct((QUAD, size + LOG_ROWS, HD), BF16),
        (mine,),
        **small,
    )
    lines = swap(group, line)
    hop(group)
    state = absorb(state, (1, 2), back[1:3])
    hop(state)
    total = call(
        group_body,
        jax.ShapeDtypeStruct((shards // span, size + 8, HD), F32),
        (lines,),
        **small,
    )
    wides = swap(total, wide)
    hop(total)
    state = absorb(state, (3, 4), back[3:5])
    hop(state)
    entering = call(
        enter_body,
        jax.ShapeDtypeStruct((QUAD, size, HD), BF16),
        (place, mine, lines, wides),
        smem=(0,),
        **small,
    )
    hop(entering)
    entering = swap(entering, near).reshape(heads, HD, HD)
    state = absorb(state, (5, 6), back[5:7])
    raw, squares = call(
        raw_body,
        (
            jax.ShapeDtypeStruct((tokens, features), F32),
            jax.ShapeDtypeStruct((peers * SAME, tokens), F32),
        ),
        (lin_query, logs, local, entering),
        flops=2 * tokens * features * HD,
        moved=10 * tokens * features,
    )
    squares = lax.all_to_all(squares, "head", 0, 0, tiled=True)
    lin_out = call(
        functools.partial(norm_body, float(features * peers)),
        jax.ShapeDtypeStruct((tokens, features), BF16),
        (raw, squares, lin_gate, norm_gain.reshape(1, features)),
        flops=8 * tokens * features,
        moved=8 * tokens * features,
        exps=tokens * features,
    )
    assert len(back) == hops + 1
    soft_out = absorb(state, tuple(range(7, hops + 1)), back[7:], True)
    return (lin_out, soft_out)


def solution(mesh):
    spread = P("seq", "head")
    return jax.shard_map(
        on_device,
        mesh=mesh,
        in_specs=(spread,) * 5 + (P("head"),) + (spread,) * 3 + (P(),),
        out_specs=(spread, spread),
        check_vma=False,
    )
```

```python
import functools
import math

import jax
import jax.numpy as jnp
import numpy as np
from jax import lax
from jax.experimental import pallas as pl
from jax.experimental.pallas import tpu as pltpu
from jax.sharding import PartitionSpec as P

HD = 128
BLK = 256
MBLK = 128
DOC_MOST = 29
EPS = 1e-06
NEG = -1e30
LOG_FLOOR = -1000.0
LOG_ROWS = 16
SAME = 8
QUAD = 4
F32 = jnp.float32
BF16 = jnp.bfloat16
VMEM_LIMIT = 8 * 1024 * 1024
ATTEND_LIMIT = 12 * 1024 * 1024
NEARLY_ALL = (64 * 1024 - 768) * 1024
WHOLE_LIMIT = (64 * 1024 - 512) * 1024
COST = 4 * 10**9


def call(
    body, outs, operands, *, flops, moved, exps=0, scratch=(), smem=(), aliases=None, after=()
):
    count = len(operands)
    if after:
        inner = body
        body = lambda *refs: inner(*refs[:count], *refs[count + len(after) :])
    operands = (*operands, *after)
    spaces = [pltpu.SMEM if i in smem else pltpu.VMEM for i in range(len(operands) - len(after))]
    specs = [pl.BlockSpec(memory_space=m) for m in spaces + [pl.ANY] * len(after)]
    return pl.pallas_call(
        body,
        out_shape=outs,
        in_specs=specs,
        out_specs=jax.tree.map(lambda _: pl.BlockSpec(memory_space=pltpu.VMEM), outs),
        scratch_shapes=list(scratch),
        input_output_aliases=aliases or {},
        compiler_params=pltpu.CompilerParams(vmem_limit_bytes=VMEM_LIMIT),
        cost_estimate=pl.CostEstimate(
            flops=int(flops), bytes_accessed=int(moved), transcendentals=int(exps)
        ),
    )(*operands)


def dot(a, b, dims, precision=None):
    return lax.dot_general(
        a, b, (dims, ((), ())), preferred_element_type=F32, precision=precision
    )


def split(x):
    high = x.astype(BF16)
    return high, (x - high.astype(F32)).astype(BF16)


def block_sums(log_ref):
    return [dot(tri, logs, ((1,), (1,)), lax.Precision.HIGHEST) for tri, logs in blocks_of(log_ref)]


def block_sums_across(log_ref):
    return [dot(logs, tri, ((1,), (1,)), lax.Precision.HIGHEST) for tri, logs in blocks_of(log_ref)]


def blocks_of(log_ref):
    rows = lax.broadcasted_iota(jnp.int32, (BLK, BLK), 0)
    cols = lax.broadcasted_iota(jnp.int32, (BLK, BLK), 1)
    tri = (rows >= cols).astype(F32)
    return [
        (tri, log_ref[:, b * BLK : (b + 1) * BLK]) for b in range(log_ref.shape[1] // BLK)
    ]


def log_rows(total):
    first = total.astype(BF16).astype(F32)
    second = (total - first).astype(BF16).astype(F32)
    third = total - first - second
    row = lax.broadcasted_iota(jnp.int32, (LOG_ROWS, HD), 0)
    packed = jnp.where(row == 0, first, jnp.where(row == 1, second, jnp.where(row == 2, third, 0.0)))
    return packed.astype(BF16)


def join_body(key_hbm, value_hbm, moving_ref, sems):
    width = key_hbm.shape[1]
    copies = [
        pltpu.make_async_copy(key_hbm, moving_ref.at[:, pl.ds(0, width)], sems.at[0]),
        pltpu.make_async_copy(value_hbm, moving_ref.at[:, pl.ds(width, width)], sems.at[1]),
    ]
    for copy in copies:
        copy.start()
    for copy in copies:
        copy.wait()


def states_body(key_hbm, value_hbm, log_hbm, *rest):
    send_ref, first_ref, key_ref, value_ref, log_ref, sems = rest[-6:]
    copies = [
        pltpu.make_async_copy(log_hbm, log_ref, sems.at[0]),
        pltpu.make_async_copy(key_hbm, key_ref, sems.at[1]),
        pltpu.make_async_copy(value_hbm, value_ref, sems.at[2]),
    ]
    for copy in copies:
        copy.start()
    for copy in copies:
        copy.wait()
    heads = key_ref.shape[1] // HD
    sums = block_sums(log_ref)
    ends = [s[BLK - 1 : BLK, :] for s in sums]
    for h in range(heads):
        lanes = slice(h * HD, (h + 1) * HD)
        state = None
        total = jnp.zeros((1, 1), F32)
        for b, cum in enumerate(sums):
            rows = slice(b * BLK, (b + 1) * BLK)
            end = ends[b][:, h : h + 1]
            weight = jnp.exp(end - cum[:, h : h + 1])
            high, low = split(key_ref[rows, lanes].astype(F32) * weight)
            value = value_ref[rows, lanes]
            local = dot(high, value, ((0,), (0,))) + dot(low, value, ((0,), (0,)))
            if b == 0:
                first_ref[h] = local
                state = local
            else:
                state = jnp.exp(end) * state + local
            total = total + end
        total = jnp.broadcast_to(jnp.maximum(total, LOG_FLOOR), (1, HD))
        share, size = send_ref.shape[0] // heads, send_ref.shape[1] - LOG_ROWS
        for j in range(share):
            send_ref[h * share + j, :size, :] = state[j * size : (j + 1) * size].astype(BF16)
            send_ref[h * share + j, size:, :] = log_rows(total)


def local_body(query_ref, key_ref, value_ref, log_ref, first_ref, raw_ref):
    heads = key_ref.shape[1] // HD
    sums = block_sums(log_ref)
    across = block_sums_across(log_ref)
    rows_i = lax.broadcasted_iota(jnp.int32, (BLK, BLK), 0)
    cols_i = lax.broadcasted_iota(jnp.int32, (BLK, BLK), 1)
    causal = rows_i >= cols_i
    for b, cum in enumerate(sums):
        rows = slice(b * BLK, (b + 1) * BLK)
        for h in range(heads):
            lanes = slice(h * HD, (h + 1) * HD)
            column = cum[:, h : h + 1]
            query = query_ref[rows, lanes]
            gap = column - across[b][h : h + 1, :]
            weight = jnp.exp(jnp.where(causal, gap, NEG))
            scores = dot(query, key_ref[rows, lanes], ((1,), (1,)))
            mixed = (scores * weight).astype(BF16)
            raw = dot(mixed, value_ref[rows, lanes], ((1,), (0,)))
            if b > 0:
                high, low = split(first_ref[h])
                inter = dot(query, high, ((1,), (0,))) + dot(query, low, ((1,), (0,)))
                raw = raw + jnp.exp(column) * inter
            raw_ref[rows, lanes] = raw


def fold(parts):
    state, total = parts[0]
    for s, l in parts[1:]:
        state = jnp.exp(l) * state + s
        total = total + l
    return state, jnp.maximum(total, LOG_FLOOR)


def parts_of(got_ref, size):
    return [
        (
            got_ref[j, :size, :].astype(F32),
            jnp.sum(got_ref[j, size:, :].astype(F32), axis=0, keepdims=True),
        )
        for j in range(got_ref.shape[0])
    ]


def group_body(got_ref, send_ref):
    size = got_ref.shape[1] - LOG_ROWS
    state, total = fold(parts_of(got_ref, size))
    state = state.astype(send_ref.dtype)
    if send_ref.dtype == F32:
        row = lax.broadcasted_iota(jnp.int32, (send_ref.shape[1] - size, HD), 0)
        rows = jnp.where(row == 0, total, 0.0)
    else:
        rows = log_rows(total)
    for j in range(send_ref.shape[0]):
        send_ref[j, :size, :] = state
        send_ref[j, size:, :] = rows


def before(parts, place):
    state = jnp.zeros_like(parts[0][0])
    for j, (s, l) in enumerate(parts[:-1]):
        state = jnp.where(j < place, jnp.exp(l) * state + s, state)
    return state


def log_before(parts, place):
    total = jnp.zeros_like(parts[0][1])
    for j, (_, l) in enumerate(parts[:-1]):
        total = jnp.where(j < place, total + l, total)
    return total


def enter_body(place_ref, mine_ref, line_ref, wide_ref, send_ref):
    size = send_ref.shape[1]
    line = parts_of(line_ref, size)
    state = before(parts_of(wide_ref, size), place_ref[0])
    entering = jnp.exp(log_before(line, place_ref[2])) * state + before(line, place_ref[2])
    for j, (s, l) in enumerate(parts_of(mine_ref, size)):
        send_ref[j] = entering.astype(BF16)
        entering = jnp.exp(l) * entering + s


def raw_body(query_ref, log_ref, local_ref, enter_ref, raw_ref, square_ref):
    heads = query_ref.shape[1] // HD
    sums = block_sums(log_ref)
    ahead = jnp.zeros((1, heads), F32)
    for b, cum in enumerate(sums):
        rows = slice(b * BLK, (b + 1) * BLK)
        for h in range(heads):
            lanes = slice(h * HD, (h + 1) * HD)
            inter = dot(query_ref[rows, lanes], enter_ref[h], ((1,), (0,)))
            weight = jnp.exp(cum[:, h : h + 1] + ahead[:, h : h + 1])
            raw_ref[rows, lanes] = local_ref[rows, lanes] + weight * inter
        ahead = ahead + cum[BLK - 1 : BLK, :]
    raw = raw_ref[...]
    ones = jnp.ones((square_ref.shape[0], raw.shape[1]), F32)
    square_ref[...] = dot(ones, raw * raw, ((1,), (1,)), lax.Precision.HIGHEST)


def norm_body(columns, raw_ref, square_ref, gate_ref, gain_ref, out_ref):
    ones = jnp.full((square_ref.shape[0], HD), 1.0 / SAME, F32)
    total = dot(square_ref[...], ones, ((0,), (0,)), lax.Precision.HIGHEST)
    scale = lax.rsqrt(total / columns + EPS)
    for h in range(raw_ref.shape[1] // HD):
        lanes = slice(h * HD, (h + 1) * HD)
        gate = jax.nn.sigmoid(gate_ref[:, lanes].astype(F32))
        out_ref[:, lanes] = (raw_ref[:, lanes] * scale * gain_ref[:, lanes] * gate).astype(BF16)


def states(lin_key, lin_value, log_decay, soft_key, soft_value):
    tokens, features = lin_key.shape
    heads = features // HD
    logs = log_decay.T
    anywhere = pl.BlockSpec(memory_space=pl.ANY)
    vectors = pl.BlockSpec(memory_space=pltpu.VMEM)
    limit = pltpu.CompilerParams(vmem_limit_bytes=WHOLE_LIMIT)
    moving = pl.pallas_call(
        join_body,
        out_shape=jax.ShapeDtypeStruct((tokens, 2 * soft_key.shape[1]), BF16),
        in_specs=[anywhere] * 2,
        out_specs=vectors,
        scratch_shapes=[pltpu.SemaphoreType.DMA((2,))],
        compiler_params=limit,
        cost_estimate=pl.CostEstimate(
            flops=0, bytes_accessed=8 * soft_key.size, transcendentals=0
        ),
    )(soft_key, soft_value)
    send, first = pl.pallas_call(
        states_body,
        out_shape=(
            jax.ShapeDtypeStruct((QUAD, heads * HD // QUAD + LOG_ROWS, HD), BF16),
            jax.ShapeDtypeStruct((heads, HD, HD), F32),
        ),
        in_specs=[anywhere] * 4,
        out_specs=(vectors, vectors),
        scratch_shapes=[
            pltpu.VMEM((tokens, features), BF16),
            pltpu.VMEM((tokens, features), BF16),
            pltpu.VMEM(logs.shape, F32),
            pltpu.SemaphoreType.DMA((3,)),
        ],
        compiler_params=limit,
        cost_estimate=pl.CostEstimate(
            flops=4 * tokens * features * HD,
            bytes_accessed=4 * tokens * features,
            transcendentals=0,
        ),
    )(lin_key, lin_value, logs, moving)
    return logs, send, first, moving


def swap(array, groups):
    return lax.all_to_all(array, "seq", 0, 0, axis_index_groups=groups, tiled=True)


def gate_body(*refs):
    pass


def gate(array, *after):
    anywhere = pl.BlockSpec(memory_space=pl.ANY)
    return pl.pallas_call(
        gate_body,
        out_shape=jax.ShapeDtypeStruct(array.shape, array.dtype),
        in_specs=[anywhere] * (1 + len(after)),
        out_specs=anywhere,
        input_output_aliases={0: 0},
        compiler_params=pltpu.CompilerParams(vmem_limit_bytes=1024 * 1024),
        cost_estimate=pl.CostEstimate(flops=0, bytes_accessed=0, transcendentals=0),
    )(array, *after)


SCALE = math.log2(math.e) * HD ** (-0.5)


def attend_body(backs, opening, final, *refs):
    place_ref, docs_ref, query_hbm = refs[:3]
    pieces = refs[3 : 3 + len(backs)]
    rest = refs[3 + len(backs) :]
    acc_hbm = None if opening else rest[0]
    query_ref, acc_ref, query_sem, in_sem, out_sem = rest[-5:]
    out_ref = rest[-6] if final else rest[-7]
    if not final:
        rest[-6][...] = jnp.zeros_like(rest[-6])
    tokens, features = query_hbm.shape
    heads = features // HD
    blocks = tokens // MBLK
    rows = heads * MBLK
    shard = place_ref[1]

    begins = []
    for i in range(blocks):
        mine = docs_ref[shard * blocks + i]
        begins.append([])
        for back in backs:
            start = jnp.int32(0)
            for b in range(i if back == 0 else blocks):
                where = (shard - back) * blocks + b
                other = docs_ref[jnp.maximum(where, 0)]
                start = start + jnp.where((where >= 0) & (other == mine), 0, MBLK)
            begins[i].append(start)
    reached = [functools.reduce(jnp.minimum, starts) < tokens for starts in begins]

    def query_copy(i):
        return pltpu.make_async_copy(
            query_hbm.at[pl.ds(i * MBLK, MBLK), :], query_ref.at[i], query_sem.at[i]
        )

    def in_copy(i):
        return pltpu.make_async_copy(acc_hbm.at[i], acc_ref.at[i], in_sem.at[i])

    def out_copy(i):
        return pltpu.make_async_copy(acc_ref.at[i], out_ref.at[i], out_sem.at[i])

    for i in range(blocks):
        if final:
            in_copy(i).start()

        @pl.when(reached[i])
        def _():
            query_copy(i).start()
            if not opening and not final:
                in_copy(i).start()

    for i in range(blocks):
        if final:
            in_copy(i).wait()

        @pl.when(reached[i])
        def _():
            query_copy(i).wait()
            if not opening and not final:
                in_copy(i).wait()

        def queries():
            return jnp.concatenate(
                [query_ref[i, :, h * HD : (h + 1) * HD] for h in range(heads)], axis=0
            )

        for back, piece, start in zip(backs, pieces, begins[i]):
            if back == 0:
                width = (i + 1) * MBLK
                scores = dot(piece[:width, :HD], queries(), ((1,), (1,)))
                key = lax.broadcasted_iota(jnp.int32, (width, rows), 0)
                token = lax.broadcasted_iota(jnp.int32, (width, rows), 1)
                token = (token & (MBLK - 1)) + i * MBLK
                scores = jnp.where((key <= token) & (key >= start), scores, NEG)
                top = jnp.max(scores, axis=0, keepdims=True)
                probs = jnp.exp2(scores * SCALE - top * SCALE)
                total = jnp.sum(probs, axis=0, keepdims=True)
                acc_ref[i, :HD, :] = dot(piece[:width, HD:], probs.astype(BF16), ((0,), (0,)))
                acc_ref[i, HD : HD + 8, :] = jnp.broadcast_to(top, (8, rows))
                acc_ref[i, HD + 8 :, :] = jnp.broadcast_to(total, (8, rows))
                continue

            def add(masked):
                scores = dot(piece[:, :HD], queries(), ((1,), (1,)))
                if masked:
                    key = lax.broadcasted_iota(jnp.int32, (tokens, rows), 0)
                    scores = jnp.where(key >= start, scores, NEG)
                old = acc_ref[i, HD : HD + 1, :]
                top = jnp.maximum(old, jnp.max(scores, axis=0, keepdims=True))
                probs = jnp.exp2(scores * SCALE - top * SCALE)
                shrink = jnp.exp2((old - top) * SCALE)
                total = acc_ref[i, HD + 8 : HD + 9, :] * shrink + jnp.sum(
                    probs, axis=0, keepdims=True
                )
                added = dot(piece[:, HD:], probs.astype(BF16), ((0,), (0,)))
                acc_ref[i, :HD, :] = acc_ref[i, :HD, :] * shrink + added
                acc_ref[i, HD : HD + 8, :] = jnp.broadcast_to(top, (8, rows))
                acc_ref[i, HD + 8 :, :] = jnp.broadcast_to(total, (8, rows))

            pl.when(start == 0)(functools.partial(add, False))
            pl.when((start > 0) & (start < tokens))(functools.partial(add, True))

        if final:
            done = (acc_ref[i, :HD, :] / acc_ref[i, HD + 8 : HD + 9, :]).T
            for h in range(heads):
                out_ref[i * MBLK : (i + 1) * MBLK, h * HD : (h + 1) * HD] = done[
                    h * MBLK : (h + 1) * MBLK
                ].astype(BF16)
        else:

            @pl.when(reached[i])
            def _():
                out_copy(i).start()

    if not final:
        for i in range(blocks):

            @pl.when(reached[i])
            def _():
                out_copy(i).wait()


def forward(array, steps):
    shards = lax.axis_size("seq")
    return lax.ppermute(array, "seq", [(s, s + steps) for s in range(shards - steps)])


def absorber(soft_query, doc_ids, place):
    tokens, features = soft_query.shape
    blocks = tokens // MBLK
    heads = features // HD
    rows = heads * MBLK
    carry = jax.ShapeDtypeStruct((blocks, HD + 16, rows), F32)
    mark = jax.ShapeDtypeStruct((8, HD), F32)
    anywhere = pl.BlockSpec(memory_space=pl.ANY)
    scalars = pl.BlockSpec(memory_space=pltpu.SMEM)
    vectors = pl.BlockSpec(memory_space=pltpu.VMEM)

    def absorb(state, backs, arrays, final=False):
        opening = state is None
        held = [] if opening else [state]
        return pl.pallas_call(
            functools.partial(attend_body, backs, opening, final),
            out_shape=jax.ShapeDtypeStruct((tokens, features), BF16) if final else (carry, mark),
            in_specs=[scalars] * 2
            + [anywhere]
            + [vectors] * len(backs)
            + [anywhere] * len(held),
            out_specs=vectors if final else (anywhere, vectors),
            scratch_shapes=[
                pltpu.VMEM((blocks, MBLK, features), BF16),
                pltpu.VMEM(carry.shape, F32),
                pltpu.SemaphoreType.DMA((blocks,)),
                pltpu.SemaphoreType.DMA((blocks,)),
                pltpu.SemaphoreType.DMA((blocks,)),
            ],
            input_output_aliases={3 + len(backs): 0} if held and not final else {},
            compiler_params=pltpu.CompilerParams(vmem_limit_bytes=ATTEND_LIMIT if final else NEARLY_ALL),
            cost_estimate=pl.CostEstimate(
                flops=len(backs) * COST,
                bytes_accessed=12 * tokens * features,
                transcendentals=len(backs) * heads * tokens * tokens,
            ),
        )(place, doc_ids, soft_query, *arrays, *held)

    return absorb


def on_device(
    lin_query,
    lin_key,
    lin_value,
    lin_gate,
    log_decay,
    norm_gain,
    soft_query,
    soft_key,
    soft_value,
    doc_ids,
):
    tokens, features = lin_query.shape
    heads = features // HD
    shards = lax.axis_size("seq")
    peers = lax.axis_size("head")
    shard = lax.axis_index("seq")
    span = QUAD * QUAD
    place = jnp.stack([shard // span, shard, (shard % span) // QUAD]).astype(jnp.int32)
    near = [[QUAD * g + j for j in range(QUAD)] for g in range(shards // QUAD)]
    line = [
        [span * x + QUAD * a + b for a in range(QUAD)]
        for x in range(shards // span)
        for b in range(QUAD)
    ]
    wide = [[span * x + r for x in range(shards // span)] for r in range(span)]
    size = heads * HD // QUAD
    small = dict(flops=10 * heads * HD * HD, moved=4 * heads * HD * HD)
    hops = (DOC_MOST + tokens // MBLK - 2) // (tokens // MBLK)
    absorb = absorber(soft_query, doc_ids, place)

    logs, send, first, own = states(lin_key, lin_value, log_decay, soft_key, soft_value)
    mine = swap(send, near)
    back = [own]

    def hop(*after):
        if after:
            back[-1] = gate(back[-1], *after)
        back.append(forward(back[-1], 1))

    hop()
    local = call(
        local_body,
        jax.ShapeDtypeStruct((tokens, features), F32),
        (lin_query, lin_key, lin_value, logs, first),
        flops=4 * tokens * features * BLK,
        moved=10 * tokens * features,
    )
    state, mark = absorb(None, (0,), back[:1])
    hop(local, mark)
    group = call(
        group_body,
        jax.ShapeDtypeStruct((QUAD, size + LOG_ROWS, HD), BF16),
        (mine,),
        **small,
    )
    lines = swap(group, line)
    hop(group)
    state, mark = absorb(state, (1, 2), back[1:3])
    hop(mark)
    total = call(
        group_body,
        jax.ShapeDtypeStruct((shards // span, size + 8, HD), F32),
        (lines,),
        **small,
    )
    wides = swap(total, wide)
    hop(total)
    state, mark = absorb(state, (3, 4), back[3:5])
    hop(mark)
    entering = call(
        enter_body,
        jax.ShapeDtypeStruct((QUAD, size, HD), BF16),
        (place, mine, lines, wides),
        smem=(0,),
        **small,
    )
    hop(entering)
    entering = swap(entering, near).reshape(heads, HD, HD)
    state, mark = absorb(state, (5, 6), back[5:7])
    raw, squares = call(
        raw_body,
        (
            jax.ShapeDtypeStruct((tokens, features), F32),
            jax.ShapeDtypeStruct((peers * SAME, tokens), F32),
        ),
        (lin_query, logs, local, entering),
        flops=2 * tokens * features * HD,
        moved=10 * tokens * features,
    )
    squares = lax.all_to_all(squares, "head", 0, 0, tiled=True)
    lin_out = call(
        functools.partial(norm_body, float(features * peers)),
        jax.ShapeDtypeStruct((tokens, features), BF16),
        (raw, squares, lin_gate, norm_gain.reshape(1, features)),
        flops=8 * tokens * features,
        moved=8 * tokens * features,
        exps=tokens * features,
    )
    assert len(back) == hops + 1
    soft_out = absorb(state, tuple(range(7, hops + 1)), back[7:], True)
    return (lin_out, soft_out)


def solution(mesh):
    spread = P("seq", "head")
    return jax.shard_map(
        on_device,
        mesh=mesh,
        in_specs=(spread,) * 5 + (P("head"),) + (spread,) * 3 + (P(),),
        out_specs=(spread, spread),
        check_vma=False,
    )
```
